128 devices in a mesh: coarse: 8 (over y, z_lo), fine: 16 (over x, z_hi, core).
Axes of the slice: x: 4, y: 4, z: 4 (z_hi: 2, z_lo: 2; z = z_hi * 2 + z_lo), core: 2. Of those that a mesh axis runs over, the one named last changes fastest.
Arguments:
- field_in: float32 [512, 2, 256, 256], P(('coarse', 'fine')), may hold values from -6 to 6
- phases: float32 [512, 1024], P(('coarse', 'fine')), may hold values from -3.140625 to 3.140625
- energy: float32 [512, 1024], P(('coarse', 'fine')), may hold values from -4 to 4
- cell_index: int32 [512, 2, 1024], P(('coarse', 'fine')), may hold values from 0 to 255
- offsets: float32 [512, 2, 1024], P(('coarse', 'fine')), may hold values from -0.5 to 0.5
- slip_plan: int32 [4], replicated, may hold values from 1 to 2, as said below
- bragg_response: float32 [2, 512], replicated, may hold values from -1 to 1
Outputs:
- field_out: float32 [512, 2, 256, 256], P(('coarse', 'fine'))
- particles: float32 [512, 2, 1024], P(('coarse', 'fine'))
The draws below stay inside these ranges and needn't reach their ends.
Inputs may be any that keep to these rules, and one draw needn't show every extreme that they name: `slip_plan`: each undulator step slips the field by 1 or 2 slices; at least one step slips by 1 and at least one by 2.
All inputs are finite; a program needn't handle non-finite values.
Results may differ from the reference program's by a relative error of at most 0.0065.
Values sent between devices are 32-bit elements; how exact they have to be, the bound alone decides.
A program may use at most 192 MiB of HBM per device.

```python
import math
import jax
import jax.numpy as jnp
from jax import lax

W = 256
P_SIZE = 1024
STEPS = 4
NS = 512


def draw_slip_plan(key, part):
    key_base, key_first, key_second = jax.random.split(key, 3)
    position = jnp.arange(STEPS, dtype=jnp.int32)
    base_values = jax.random.randint(key_base, (STEPS,), 1, 3).astype(jnp.int32)
    first_slot = jax.random.randint(key_first, (), 0, STEPS).astype(jnp.int32)
    second_slot = ((first_slot + 1 + jax.random.randint(key_second, (), 0, STEPS - 1)) % STEPS).astype(jnp.int32)
    return jnp.where(position == first_slot, 1, jnp.where(position == second_slot, 2, base_values)).astype(jnp.int32)


def place_ends(drawn, key, low, top_value):
    shape = drawn.shape
    place = [jax.random.randint(jax.random.fold_in(key, axis), (), 0, shape[axis]) for axis in range(len(shape))]
    drawn = drawn.at[tuple(place)].set(low)
    longest = shape.index(max(shape))
    place[longest] = (place[longest] + 1) % shape[longest]
    return drawn.at[tuple(place)].set(top_value)


def shard_levels(own_key, shape, pieces, low, top_value):
    loudness = 1.0
    for dim, blocks in pieces:
        heights = jax.random.uniform(jax.random.fold_in(jax.random.fold_in(own_key, 6), dim), (blocks,), jnp.float32, low / len(pieces), top_value / len(pieces))
        loudness = loudness * jnp.repeat(jnp.exp(heights), shape[dim] // blocks).reshape((-1,) + (1,) * (len(shape) - 1 - dim))
    return loudness


def bell_draw(rng, shape, width, bound, cuts=(), kind=jnp.bfloat16):
    values = width * jax.random.normal(rng, shape, jnp.float32)
    if cuts:
        values = values * shard_levels(rng, shape, cuts, -0.22, 0.18)
    return jnp.clip(values, -bound, bound).astype(kind)


def setup_inputs(seed: int = 0) -> dict:
    seeds = jax.random.split(jax.random.key(seed), 8)
    return {
        "field_in": bell_draw(seeds[0], (NS, 2, W, W), 1.0, 6.0, ((0, 128),), jnp.float32),
        "phases": jnp.clip(jax.random.uniform(seeds[1], (NS, P_SIZE), jnp.float32, -3.140625, 3.140625), -3.140625, 3.140625),
        "energy": bell_draw(seeds[2], (NS, P_SIZE), 1.0, 4.0, ((0, 128),), jnp.float32),
        "cell_index": place_ends(jax.random.randint(seeds[3], (NS, 2, P_SIZE), 0, W), jax.random.fold_in(seeds[3], 1), 0, W - 1).astype(jnp.int32),
        "offsets": jnp.clip(jax.random.uniform(seeds[4], (NS, 2, P_SIZE), jnp.float32, -0.5, 0.5) * shard_levels(seeds[4], (NS, 2, P_SIZE), ((0, 128),), -0.4, 0.0), -0.5, 0.5),
        "slip_plan": draw_slip_plan(jax.random.fold_in(seeds[7], 71), 0),
        "bragg_response": jnp.clip(jax.random.uniform(seeds[6], (2, NS), jnp.float32, -1.0, 1.0), -1.0, 1.0),
    }


coupling = 0.25
push_gain = 0.5
phase_rate = 1.0
spread_cells = 20.0


def spline_weights(offsets):
    left_weight = 0.5 * (0.5 - offsets) * (0.5 - offsets)
    middle_weight = 0.75 - offsets * offsets
    right_weight = 0.5 * (0.5 + offsets) * (0.5 + offsets)
    return jnp.stack([left_weight, middle_weight, right_weight], axis=-1).astype(jnp.bfloat16)


def propagator_kernel(extent):
    frequency = jnp.arange(extent, dtype=jnp.int32)
    signed = jnp.where(frequency < extent // 2, frequency, frequency - extent).astype(jnp.float32)
    angles = -spread_cells * (2.0 * math.pi * signed / extent) ** 2
    return jnp.cos(angles) + 1j * jnp.sin(angles)


def segment_row(term_row, index_row):
    return jax.ops.segment_sum(term_row, index_row, num_segments=W * W)


def reference(field_in, phases, energy, cell_index, offsets, slip_plan, bragg_response):
    strides = jnp.array([-1, 0, 1], dtype=jnp.int32)
    weight_x = spline_weights(offsets[:, 0]).astype(jnp.float32)
    weight_y = spline_weights(offsets[:, 1]).astype(jnp.float32)
    column_x = (cell_index[:, 0, :, None] + strides) % W
    column_y = (cell_index[:, 1, :, None] + strides) % W
    flat_index = (column_x[:, :, :, None] * W + column_y[:, :, None, :]).reshape(NS, P_SIZE * 9).astype(jnp.int32)
    pair_weight = weight_x[:, :, :, None] * weight_y[:, :, None, :]
    kernel = propagator_kernel(W)
    spectral = kernel[:, None] * kernel[None, :]
    deposit_gain = coupling * W * W / P_SIZE
    field_now = field_in
    for undulator in range(STEPS):
        cosine = jnp.cos(phases)
        sine_part = jnp.sin(phases)
        deposits = []
        for factor in (cosine, -sine_part):
            scaled = lax.optimization_barrier((weight_x * factor[:, :, None]).astype(jnp.bfloat16)).astype(jnp.float32)
            term_rows = (scaled[:, :, :, None] * weight_y[:, :, None, :]).reshape(NS, P_SIZE * 9)
            summed = jax.vmap(segment_row)(term_rows, flat_index)
            deposits.append(summed.reshape(NS, W, W))
        current = jnp.stack(deposits, axis=1)
        field_now = field_now + deposit_gain * current
        complex_field = field_now[:, 0] + 1j * field_now[:, 1]
        complex_field = jnp.fft.ifft2(jnp.fft.fft2(complex_field, axes=(1, 2)) * spectral, axes=(1, 2))
        field_now = jnp.stack([jnp.real(complex_field), jnp.imag(complex_field)], axis=1).astype(jnp.float32)
        rounded = lax.optimization_barrier(field_now.astype(jnp.bfloat16)).astype(jnp.float32).reshape(NS, 2, W * W)
        sampled = []
        for part_index in range(2):
            picked = jnp.take_along_axis(rounded[:, part_index], flat_index, axis=1).reshape(NS, P_SIZE, 3, 3)
            sampled.append(jnp.sum(picked * pair_weight, axis=(2, 3)))
        energy = energy - push_gain * (sampled[0] * cosine - sampled[1] * sine_part)
        phases = phases + phase_rate * energy
        padding = jnp.zeros((2, 2, W, W), jnp.float32)
        extended = jnp.concatenate([padding, field_now], axis=0)
        begin_row = (2 - slip_plan[undulator]).astype(jnp.int32)
        field_now = lax.dynamic_slice_in_dim(extended, begin_row, NS, 0)
    complex_field = field_now[:, 0] + 1j * field_now[:, 1]
    response = bragg_response[0] + 1j * bragg_response[1]
    spectrum = jnp.fft.fft(complex_field, axis=0) * response[:, None, None]
    complex_field = jnp.fft.ifft(spectrum, axis=0)
    field_out = jnp.stack([jnp.real(complex_field), jnp.imag(complex_field)], axis=1).astype(jnp.float32)
    particles = jnp.stack([phases, energy], axis=1)
    return field_out, particles
```

```python
import functools
import itertools

import jax
import jax.numpy as jnp
import numpy as np
from jax import lax
from jax.experimental import pallas as pl
from jax.experimental.pallas import tpu as pltpu
from jax.sharding import PartitionSpec as P

W = 256
HALF = 128
P_SIZE = 1024
STEPS = 4
NS = 512
CHAINS = 4
COARSE = 8
FINE = 16
DEVICES = COARSE * FINE
REACH = 10
GAIN = 0.25 * W * W / P_SIZE
SPREAD = 20.0
MESH = pl.DeviceIdType.MESH
f32, bf16 = jnp.float32, jnp.bfloat16


def halves(matrix):
    high = matrix.astype(np.float32).astype(bf16)
    low = (matrix - high.astype(np.float64)).astype(np.float32).astype(bf16)
    return high, low


def diffraction_tables():
    k = np.arange(W)
    signed = np.where(k < W // 2, k, k - W)
    h = np.exp(-1j * SPREAD * (2.0 * np.pi * signed / W) ** 2)
    q = np.fft.ifft(h)
    full = q[(k[:, None] - k[None, :]) % W]
    a, b = full[:HALF, :HALF], full[:HALF, HALF:]
    right, left = [], []
    for part in (0.5 * (a + b), 0.5 * (a - b)):
        t = part.T
        hi, lo = halves(np.block([[t.real, t.imag], [-t.imag, t.real]]))
        right.append(np.concatenate([hi, lo, hi], axis=0))
        hi, lo = halves(np.block([[part.real, -part.imag], [part.imag, part.real]]))
        left.append(np.concatenate([hi, hi, lo], axis=1))
    return np.stack(right), np.stack(left)


def time_tables():
    m = np.arange(NS // 2)
    t = np.arange(NS // 2)
    tables = []
    for parity in (0, 1):
        angle = 2.0 * np.pi * ((2 * m[:, None] + parity) * t[None, :] % NS) / NS
        c, s = np.cos(angle), np.sin(angle)
        full = np.stack([np.stack([c, s], 1), np.stack([-s, c], 1)], 0)
        full = full.reshape(2, NS // 2, 2, NS // 8, CHAINS).transpose(0, 1, 3, 2, 4).reshape(NS, NS)
        tables.append(np.stack(halves(full)))
    return np.stack(tables)


def place(n):
    n = lax.rem(n + 2 * DEVICES, DEVICES)
    return (n // FINE, lax.rem(n, FINE))


def my_index():
    return lax.axis_index("coarse") * FINE + lax.axis_index("fine")


def sincos(x):
    turns = jnp.round(x * (2.0 / np.pi))
    r = x - turns * 1.5703125
    r = r - turns * 4.837512969970703125e-4
    r = r - turns * 7.54978995489188216e-8
    z = r * r
    sine = r + r * z * (-1.6666654611e-1 + z * (8.3321608736e-3 + z * -1.9515295891e-4))
    cosine = 1.0 - 0.5 * z + z * z * (4.166664568298827e-2 + z * (-1.388731625493765e-3 + z * 2.443315711809948e-5))
    quadrant = turns.astype(jnp.int32) & 3
    odd = (quadrant & 1) == 1
    s = jnp.where(odd, cosine, sine)
    c = jnp.where(odd, sine, cosine)
    s = jnp.where(quadrant >= 2, -s, s)
    c = jnp.where((quadrant == 1) | (quadrant == 2), -c, c)
    return s, c


def spline_rows(table, r, cells, shifts):
    near = shifts
    left = (0.5 * (0.5 - near) * (0.5 - near)).astype(bf16).astype(f32)
    middle = (0.75 - near * near).astype(bf16).astype(f32)
    right = (0.5 * (0.5 + near) * (0.5 + near)).astype(bf16).astype(f32)
    before = (cells - 1) & (W - 1)
    after = (cells + 1) & (W - 1)
    step = 32
    for row in range(0, W, step):
        grid = lax.broadcasted_iota(jnp.int32, (step, P_SIZE), 0) + row
        value = jnp.where(grid == before, left, 0.0)
        value = jnp.where(grid == cells, middle, value)
        value = jnp.where(grid == after, right, value)
        table[r, row : row + step, :] = value.astype(bf16)


def steps_kernel(
    slip, field_in, phases, energy, cells, shifts, mright, mleft, out, ends,
    field, tx, ty, gcells, gshifts, state, arrived, dep, cur, lhs, rhs, rounded,
    load_sem, gs, gr, ps, pr,
):
    me = my_index()
    barrier = pltpu.get_barrier_semaphore()
    for step in (-2, -1, 1, 2):
        pl.semaphore_signal(barrier, inc=1, device_id=place(me + step), device_id_type=MESH)
    load = pltpu.make_async_copy(field_in, field, load_sem)
    load.start()
    gcells[0:CHAINS] = cells[...]
    gshifts[0:CHAINS] = shifts[...]
    pl.semaphore_wait(barrier, 4)
    sends = []
    for n, (src, dst) in enumerate(((cells, gcells), (shifts, gshifts))):
        sends.append(pltpu.make_async_remote_copy(
            src, dst.at[pl.ds(4, 4)], gs.at[n], gr.at[n], device_id=place(me - 1), device_id_type=MESH))
        sends.append(pltpu.make_async_remote_copy(
            src.at[pl.ds(0, 2)], dst.at[pl.ds(8, 2)], gs.at[n + 2], gr.at[n + 2], device_id=place(me - 2), device_id_type=MESH))
    for copy in sends:
        copy.start()

    def build(r, carry):
        spline_rows(tx, r, gcells[r, 0:1, :], gshifts[r, 0:1, :])
        spline_rows(ty, r, gcells[r, 1:2, :], gshifts[r, 1:2, :])
        return carry

    lax.fori_loop(0, CHAINS, build, 0)
    for copy in sends:
        copy.wait()
    lax.fori_loop(CHAINS, REACH, build, 0)
    load.wait()

    def pair(u, base, theta, eta):
        met = slip[STEPS + u]
        sine, cosine = sincos(theta)
        for k in range(2):
            r = base + k + met
            c, s = cosine[k : k + 1], -sine[k : k + 1]
            for row in range(0, W, 32):
                weights = tx[r, row : row + 32, :].astype(f32)
                dep[k, row : row + 32, :] = (weights * c).astype(bf16)
                dep[k, W + row : W + row + 32, :] = (weights * s).astype(bf16)
            cur[k] = lax.dot_general(dep[k], ty[r], (((1,), (1,)), ((), ())), preferred_element_type=f32)
        for k in range(2):
            chain = base + k
            at = me * CHAINS + chain
            fresh = (at + met >= NS) & (at + slip[2 * STEPS + u] < NS)
            keep = jnp.where(fresh, 0.0, 1.0)
            for c in range(2):
                for row in range(0, HALF, 32):
                    top = field[chain, c, row : row + 32, :] * keep + GAIN * cur[k, c * W + row : c * W + row + 32, :]
                    low = row + HALF
                    bottom = field[chain, c, low : low + 32, :] * keep + GAIN * cur[k, c * W + low : c * W + low + 32, :]
                    for sx, v in enumerate((top + bottom, top - bottom)):
                        a, b = v[:, :HALF], v[:, HALF:]
                        rows = slice(sx * HALF + row, sx * HALF + row + 32)
                        for sy, g in enumerate((a + b, a - b)):
                            hi = g.astype(bf16)
                            lo = (g - hi.astype(f32)).astype(bf16)
                            lhs[k, sy, rows, c * HALF : c * HALF + HALF] = hi
                            lhs[k, sy, rows, W + c * HALF : W + c * HALF + HALF] = hi
                            lhs[k, sy, rows, 2 * W + c * HALF : 2 * W + c * HALF + HALF] = lo
            for sy in range(2):
                mid = jnp.dot(lhs[k, sy], mright[sy], preferred_element_type=f32)
                for sx in range(2):
                    for c in range(2):
                        g = mid[sx * HALF : sx * HALF + HALF, c * HALF : c * HALF + HALF]
                        hi = g.astype(bf16)
                        lo = (g - hi.astype(f32)).astype(bf16)
                        cols = slice(sy * HALF, sy * HALF + HALF)
                        rhs[k, sx, c * HALF : c * HALF + HALF, cols] = hi
                        rhs[k, sx, W + c * HALF : W + c * HALF + HALF, cols] = lo
                        rhs[k, sx, 2 * W + c * HALF : 2 * W + c * HALF + HALF, cols] = hi
        for k in range(2):
            chain = base + k
            za = jnp.dot(mleft[0], rhs[k, 0], preferred_element_type=f32)
            zb = jnp.dot(mleft[1], rhs[k, 1], preferred_element_type=f32)
            for c in range(2):
                p, n = za[c * HALF : c * HALF + HALF], zb[c * HALF : c * HALF + HALF]
                for hx, v in enumerate((p + n, p - n)):
                    a, b = v[:, :HALF], v[:, HALF:]
                    for hy, g in enumerate((a + b, a - b)):
                        rows = slice(hx * HALF, hx * HALF + HALF)
                        cols = slice(hy * HALF, hy * HALF + HALF)
                        field[chain, c, rows, cols] = g
                        rounded[k, c * W + hx * HALF : c * W + hx * HALF + HALF, cols] = g.astype(bf16)
        sampled = []
        for k in range(2):
            r = base + k + met
            pieces = []
            for q in range(0, P_SIZE, 256):
                picked = jnp.dot(rounded[k], ty[r, :, q : q + 256], preferred_element_type=f32)
                weights = tx[r, :, q : q + 256].astype(f32)
                pieces.append([jnp.sum(picked[c * W : c * W + W] * weights, axis=0, keepdims=True) for c in range(2)])
            sampled.append([jnp.concatenate([piece[c] for piece in pieces], axis=1) for c in range(2)])
        first = jnp.concatenate([sampled[0][0], sampled[1][0]], axis=0)
        second = jnp.concatenate([sampled[0][1], sampled[1][1]], axis=0)
        eta = eta - 0.5 * (first * cosine - second * sine)
        return theta + eta, eta

    def store(u, base, theta, eta):
        state[u, 0, base : base + 2, :] = theta
        state[u, 1, base : base + 2, :] = eta

    def exchange(u):
        return [
            pltpu.make_async_remote_copy(
                state.at[u, n, pl.ds(0, 2)], arrived.at[u, n], ps.at[u, n], pr.at[u, n],
                device_id=place(me - 1), device_id_type=MESH)
            for n in range(2)
        ]

    theta, eta = phases[0:2], energy[0:2]
    moving = None
    for u in range(STEPS):
        if u:
            one = slip[u - 1] == 1
            theta, eta = (jnp.where(one, state[u - 1, n, 1:3, :], state[u - 1, n, 2:4, :]) for n in range(2))
        theta, eta = pair(u, 0, theta, eta)
        store(u, 0, theta, eta)
        if u:
            for copy in moving:
                copy.wait()
            theta, eta = (
                jnp.where(
                    one,
                    jnp.concatenate([state[u - 1, n, 3:4, :], arrived[u - 1, n, 0:1, :]], axis=0),
                    arrived[u - 1, n],
                )
                for n in range(2)
            )
        else:
            theta, eta = phases[2:4], energy[2:4]
        if u < STEPS - 1:
            moving = exchange(u)
            for copy in moving:
                copy.start()
        theta, eta = pair(u, 2, theta, eta)
        store(u, 2, theta, eta)
    for chain in range(CHAINS):
        at = me * CHAINS + chain
        gone = (at + slip[3 * STEPS] >= NS) & (at + slip[2 * STEPS - 1] < NS)
        keep = jnp.where(gone, 0.0, 1.0)
        for c in range(2):
            for hx in range(2):
                for hy in range(2):
                    out[2 * hx + hy, pl.ds(c * CHAINS + chain, HALF, stride=8), :] = (
                        field[chain, c, hx * HALF : hx * HALF + HALF, hy * HALF : hy * HALF + HALF] * keep
                    )
    ends[...] = state[STEPS - 1]


def far_first():
    offsets = [o for o in itertools.product(range(4), range(4), range(4), range(2)) if any(o)]
    mixed = np.random.RandomState(1).permutation(len(offsets))
    offsets = [offsets[i] for i in mixed]
    return sorted(offsets, key=lambda o: -sum(min(v, 4 - v) for v in o[:3]))


def partners():
    coarse, fine = lax.axis_index("coarse"), lax.axis_index("fine")
    x, y = fine // 4, coarse // 2
    z, core = (lax.rem(fine, 4) // 2) * 2 + lax.rem(coarse, 2), lax.rem(fine, 2)
    out = []
    for dx, dy, dz, dk in far_first():
        px, py, pz, pk = lax.rem(x + dx, 4), lax.rem(y + dy, 4), lax.rem(z + dz, 4), lax.rem(core + dk, 2)
        out.append((py * 2 + lax.rem(pz, 2), px * 4 + (pz // 2) * 2 + pk))
    return out


PARTS = 2
TILES = 4 // PARTS
WIDTH = TILES * HALF


def filter_kernel(
    slip, sent, ends, columns, tables, back, particles,
    table, got, result, scaled, conv, operand, homes,
    table_sem, own_sem, s1, r1, s2, r2, hs, hr,
):
    me = my_index()
    others = partners()
    barrier = pltpu.get_barrier_semaphore()
    for there in others:
        pl.semaphore_signal(barrier, inc=1, device_id=there, device_id_type=MESH)
    load = pltpu.make_async_copy(tables, table, table_sem)
    load.start()
    pl.semaphore_wait(barrier, DEVICES - 1)

    def spread(src, dst, q, ss, rs):
        tiles = pl.ds(q * TILES, TILES)
        for there in others:
            pltpu.make_async_remote_copy(
                src.at[tiles, there[0] * FINE + there[1]], dst.at[tiles, me], ss.at[q], rs.at[q],
                device_id=there, device_id_type=MESH).start()

    def settle(ref, q, sem):
        view = ref.at[pl.ds(q * TILES, TILES), pl.ds(0, DEVICES - 1)]
        pltpu.make_async_copy(view, view, sem.at[q]).wait()

    for q in range(PARTS):
        spread(sent, got, q, s1, r1)
    own = pltpu.make_async_copy(sent.at[:, me], got.at[:, me], own_sem.at[0])
    own.start()
    homing = [
        pltpu.make_async_remote_copy(
            ends, homes.at[n], hs.at[n], hr.at[n], device_id=place(me + n + 1), device_id_type=MESH)
        for n in range(2)
    ]
    for copy in homing:
        copy.start()
    load.wait()
    quarter = NS // 2
    for parity in range(2):
        re, im = columns[:, 2 * parity : 2 * parity + 1], columns[:, 2 * parity + 1 : 2 * parity + 2]
        for row in range(0, quarter, 64):
            rows, below = slice(row, row + 64), slice(quarter + row, quarter + row + 64)
            wr = table[parity, 0, rows, :].astype(f32) + table[parity, 1, rows, :].astype(f32)
            wi = table[parity, 0, below, :].astype(f32) + table[parity, 1, below, :].astype(f32)
            for start, g in (
                (row, re[rows] * wr - im[rows] * wi),
                (quarter + row, im[rows] * wr + re[rows] * wi),
            ):
                hi = g.astype(bf16)
                scaled[0, start : start + 64, :] = hi
                scaled[1, start : start + 64, :] = (g - hi.astype(f32)).astype(bf16)
        dims = (((0,), (0,)), ((), ()))
        kernel = (
            lax.dot_general(table[parity, 0], scaled[0], dims, preferred_element_type=f32)
            + lax.dot_general(table[parity, 0], scaled[1], dims, preferred_element_type=f32)
            + lax.dot_general(table[parity, 1], scaled[0], dims, preferred_element_type=f32)
        )
        hi = kernel.astype(bf16)
        conv[parity, :, 0:NS] = hi
        conv[parity, :, NS : 2 * NS] = hi
        conv[parity, :, 2 * NS : 3 * NS] = (kernel - hi.astype(f32)).astype(bf16)
    own.wait()
    mid = DEVICES // 2
    for q in range(PARTS):
        settle(got, q, r1)
        for tile in range(TILES):
            lanes = slice(tile * HALF, tile * HALF + HALF)
            for block in range(0, mid, 8):
                a = got[q * TILES + tile, block : block + 8].reshape(64, HALF)
                b = got[q * TILES + tile, mid + block : mid + block + 8].reshape(64, HALF)
                for parity, g in enumerate((a + b, a - b)):
                    hi = g.astype(bf16)
                    rows = block * 8
                    operand[parity, rows : rows + 64, lanes] = hi
                    operand[parity, NS + rows : NS + rows + 64, lanes] = (g - hi.astype(f32)).astype(bf16)
                    operand[parity, 2 * NS + rows : 2 * NS + rows + 64, lanes] = hi
        for block in range(0, NS, 256):
            even = jnp.dot(conv[0, block : block + 256, :], operand[0], preferred_element_type=f32)
            odd = jnp.dot(conv[1, block : block + 256, :], operand[1], preferred_element_type=f32)
            for tile in range(TILES):
                lanes = slice(tile * HALF, tile * HALF + HALF)
                a, b = even[:, lanes], odd[:, lanes]
                result[q * TILES + tile, block // 8 : block // 8 + 32] = (a + b).reshape(32, 8, HALF)
                result[q * TILES + tile, mid + block // 8 : mid + block // 8 + 32] = (a - b).reshape(32, 8, HALF)
        spread(result, back, q, s2, r2)
    own = pltpu.make_async_copy(result.at[:, me], back.at[:, me], own_sem.at[1])
    own.start()
    for copy in homing:
        copy.wait()
    met = slip[2 * STEPS - 1]
    for i in range(CHAINS):
        at = i - met
        for n in range(2):
            value = homes[1, n, pl.ds(jnp.clip(at + 8, 0, 3), 1), :]
            value = jnp.where(at >= -4, homes[0, n, pl.ds(jnp.clip(at + 4, 0, 3), 1), :], value)
            value = jnp.where(at >= 0, ends[n, pl.ds(jnp.clip(at, 0, 3), 1), :], value)
            particles[i, n : n + 1, :] = value
    own.wait()
    for q in range(PARTS):
        settle(got, q, s1)
        settle(got, q, s2)
        settle(got, q, r2)


def unblock_kernel(blocks, out):
    for chain in range(CHAINS):
        for c in range(2):
            for hx in range(2):
                for hy in range(2):
                    out[chain, c, hx, :, hy * HALF : hy * HALF + HALF] = blocks[
                        2 * hx + hy, pl.ds(c * CHAINS + chain, 32, stride=8), :
                    ]


def on_device(field_in, phases, energy, cell_index, offsets, slip_plan, bragg_response):
    slip_plan = slip_plan.astype(jnp.int32)
    met = jnp.concatenate([jnp.zeros((1,), jnp.int32), jnp.cumsum(slip_plan)])
    before = jnp.concatenate([jnp.zeros((1,), jnp.int32), met[: STEPS - 1]])
    slip = jnp.concatenate([slip_plan, met[:STEPS], before, met[STEPS:]])
    mright, mleft = diffraction_tables()
    vmem = pl.BlockSpec(memory_space=pltpu.VMEM)
    smem = pl.BlockSpec(memory_space=pltpu.SMEM)
    whole = pl.BlockSpec(memory_space=pl.ANY)
    dma = pltpu.SemaphoreType.DMA
    sent, ends = pl.pallas_call(
        steps_kernel,
        out_shape=(
            jax.ShapeDtypeStruct((4, DEVICES * 8, HALF), f32),
            jax.ShapeDtypeStruct((2, CHAINS, P_SIZE), f32),
        ),
        in_specs=[smem, whole] + [vmem] * 6,
        out_specs=(vmem, vmem),
        scratch_shapes=[
            pltpu.VMEM((CHAINS, 2, W, W), f32),
            pltpu.VMEM((REACH, W, P_SIZE), bf16),
            pltpu.VMEM((REACH, W, P_SIZE), bf16),
            pltpu.VMEM((REACH, 2, P_SIZE), jnp.int32),
            pltpu.VMEM((REACH, 2, P_SIZE), f32),
            pltpu.VMEM((STEPS, 2, CHAINS, P_SIZE), f32),
            pltpu.VMEM((STEPS, 2, 2, P_SIZE), f32),
            pltpu.VMEM((2, 2 * W, P_SIZE), bf16),
            pltpu.VMEM((2, 2 * W, W), f32),
            pltpu.VMEM((2, 2, W, 3 * W), bf16),
            pltpu.VMEM((2, 2, 3 * W, W), bf16),
            pltpu.VMEM((2, 2 * W, W), bf16),
            dma,
            dma((4,)),
            dma((4,)),
            dma((STEPS, 2)),
            dma((STEPS, 2)),
        ],
        compiler_params=pltpu.CompilerParams(
            collective_id=0, has_side_effects=True, vmem_limit_bytes=56 << 20
        ),
        name="steps",
    )(slip, field_in, phases, energy, cell_index, offsets, jnp.asarray(mright), jnp.asarray(mleft))

    frequency = jnp.arange(NS, dtype=jnp.int32)
    angle = (-2.0 * np.pi / NS) * (frequency * met[STEPS] % NS).astype(f32)
    turn_real, turn_quad = jnp.cos(angle) / NS, jnp.sin(angle) / NS
    real = bragg_response[0] * turn_real - bragg_response[1] * turn_quad
    quad = bragg_response[0] * turn_quad + bragg_response[1] * turn_real
    columns = jnp.stack([real.reshape(NS // 2, 2), quad.reshape(NS // 2, 2)], axis=2).reshape(NS // 2, 4)
    back, particles = pl.pallas_call(
        filter_kernel,
        out_shape=(
            jax.ShapeDtypeStruct((4, DEVICES, 8, HALF), f32),
            jax.ShapeDtypeStruct((CHAINS, 2, P_SIZE), f32),
        ),
        in_specs=[smem, whole, vmem, vmem, whole],
        out_specs=(whole, vmem),
        scratch_shapes=[
            pltpu.VMEM((2, 2, NS, NS), bf16),
            pltpu.VMEM((4, DEVICES, 8, HALF), f32),
            pltpu.VMEM((4, DEVICES, 8, HALF), f32),
            pltpu.VMEM((2, NS, NS), bf16),
            pltpu.VMEM((2, NS, 3 * NS), bf16),
            pltpu.VMEM((2, 3 * NS, WIDTH), bf16),
            pltpu.VMEM((2, 2, CHAINS, P_SIZE), f32),
            dma,
            dma((2,)),
            dma((PARTS,)),
            dma((PARTS,)),
            dma((PARTS,)),
            dma((PARTS,)),
            dma((2,)),
            dma((2,)),
        ],
        compiler_params=pltpu.CompilerParams(
            collective_id=1, has_side_effects=True, vmem_limit_bytes=40 << 20
        ),
        name="filter",
    )(slip, sent.reshape(4, DEVICES, 8, HALF), ends, columns, jnp.asarray(time_tables()))

    field_out = pl.pallas_call(
        unblock_kernel,
        grid=(4,),
        out_shape=jax.ShapeDtypeStruct((CHAINS, 2, 2, HALF, W), f32),
        in_specs=[pl.BlockSpec((4, 256, HALF), lambda i: (0, i, 0))],
        out_specs=pl.BlockSpec((CHAINS, 2, 2, 32, W), lambda i: (0, 0, 0, i, 0)),
        name="unblock",
    )(back.reshape(4, DEVICES * 8, HALF))
    return field_out.reshape(CHAINS, 2, W, W), particles


def solution(mesh):
    axes = ("coarse", "fine")
    in_specs = (
        P(axes, None, None, None),
        P(axes, None),
        P(axes, None),
        P(axes, None, None),
        P(axes, None, None),
        P(),
        P(),
    )
    out_specs = (P(axes, None, None, None), P(axes, None, None))
    return jax.shard_map(on_device, mesh=mesh, in_specs=in_specs, out_specs=out_specs, check_vma=False)
```

```python
import itertools

import jax
import jax.numpy as jnp
import numpy as np
from jax import lax
from jax.experimental import pallas as pl
from jax.experimental.pallas import tpu as pltpu
from jax.sharding import PartitionSpec as P

W = 256
HALF = 128
P_SIZE = 1024
STEPS = 4
NS = 512
CHAINS = 4
COARSE = 8
FINE = 16
DEVICES = COARSE * FINE
REACH = 10
GAIN = 0.25 * W * W / P_SIZE
SPREAD = 20.0
PARTS = 2
ROWS = 32 // PARTS
MESH = pl.DeviceIdType.MESH
f32, bf16 = jnp.float32, jnp.bfloat16


def halves(matrix):
    high = matrix.astype(np.float32).astype(bf16)
    low = (matrix - high.astype(np.float64)).astype(np.float32).astype(bf16)
    return high, low


def diffraction_tables():
    k = np.arange(W)
    signed = np.where(k < W // 2, k, k - W)
    h = np.exp(-1j * SPREAD * (2.0 * np.pi * signed / W) ** 2)
    q = np.fft.ifft(h)
    full = q[(k[:, None] - k[None, :]) % W]
    a, b = full[:HALF, :HALF], full[:HALF, HALF:]
    tables = []
    for part in (0.5 * (a + b), 0.5 * (a - b)):
        t = part.T
        tables.append(np.stack(halves(np.block([[t.real, t.imag], [-t.imag, t.real]]))))
    return np.stack(tables)


def place(n):
    n = lax.rem(n + 2 * DEVICES, DEVICES)
    return (n // FINE, lax.rem(n, FINE))


def far_first():
    offsets = [o for o in itertools.product(range(4), range(4), range(4), range(2)) if any(o)]
    mixed = np.random.RandomState(1).permutation(len(offsets))
    offsets = [offsets[i] for i in mixed]
    return sorted(offsets, key=lambda o: -sum(min(v, 4 - v) for v in o[:3]))


def partners():
    coarse, fine = lax.axis_index("coarse"), lax.axis_index("fine")
    x, y = fine // 4, coarse // 2
    z, core = (lax.rem(fine, 4) // 2) * 2 + lax.rem(coarse, 2), lax.rem(fine, 2)
    out = []
    for dx, dy, dz, dk in far_first():
        px, py, pz, pk = lax.rem(x + dx, 4), lax.rem(y + dy, 4), lax.rem(z + dz, 4), lax.rem(core + dk, 2)
        out.append((py * 2 + lax.rem(pz, 2), px * 4 + (pz // 2) * 2 + pk))
    return out


def sincos(x):
    turns = jnp.round(x * (2.0 / np.pi))
    r = x - turns * 1.5703125
    r = r - turns * 4.837512969970703125e-4
    r = r - turns * 7.54978995489188216e-8
    z = r * r
    sine = r + r * z * (-1.6666654611e-1 + z * (8.3321608736e-3 + z * -1.9515295891e-4))
    cosine = 1.0 - 0.5 * z + z * z * (4.166664568298827e-2 + z * (-1.388731625493765e-3 + z * 2.443315711809948e-5))
    quadrant = turns.astype(jnp.int32) & 3
    odd = (quadrant & 1) == 1
    s = jnp.where(odd, cosine, sine)
    c = jnp.where(odd, sine, cosine)
    s = jnp.where(quadrant >= 2, -s, s)
    c = jnp.where((quadrant == 1) | (quadrant == 2), -c, c)
    return s, c


def spline_rows(table, r, grid, cells, shifts):
    left = (0.5 * (0.5 - shifts) * (0.5 - shifts)).astype(bf16)
    middle = (0.75 - shifts * shifts).astype(bf16)
    right = (0.5 * (0.5 + shifts) * (0.5 + shifts)).astype(bf16)
    before = ((cells - 1) & (W - 1)).astype(f32).astype(bf16)
    after = ((cells + 1) & (W - 1)).astype(f32).astype(bf16)
    at = cells.astype(f32).astype(bf16)
    none = jnp.zeros((), bf16)
    for q in range(0, P_SIZE, W):
        lanes = slice(q, q + W)
        for row in range(0, W, 64):
            rows = grid[row : row + 64, :]
            value = jnp.where(rows == before[:, lanes], left[:, lanes], none)
            value = jnp.where(rows == at[:, lanes], middle[:, lanes], value)
            value = jnp.where(rows == after[:, lanes], right[:, lanes], value)
            table[r, row : row + 64, lanes] = value


def split(g):
    hi = g.astype(bf16)
    return hi, (g - hi.astype(f32)).astype(bf16)


def whole_kernel(
    plan, field_in, phases, energy, cells, shifts, bragg, matrices, back, particles,
    field, tx, ty, grid, gcells, gshifts, state, arrived, dep, cur, mright, mleft, lhs, rhs, rounded,
    sent, got, result, wave, turned, conv, operand, homes,
    field_sem, table_sem, gs, gr, ps, pr, own_sem, s1, r1, s2, r2, hs, hr,
):
    coarse, fine = lax.axis_index("coarse"), lax.axis_index("fine")
    me = coarse * FINE + fine
    others = partners()
    barrier = pltpu.get_barrier_semaphore()
    for there in others:
        pl.semaphore_signal(barrier, inc=1, device_id=there, device_id_type=MESH)
    slips = [plan[u] for u in range(STEPS)]
    met = [0]
    for u in range(STEPS):
        met.append(met[u] + slips[u])

    load = pltpu.make_async_copy(field_in, field, field_sem)
    load.start()
    tables = []
    for sy in range(2):
        for n, part in enumerate((0, 1, 0)):
            tables.append(pltpu.make_async_copy(
                matrices.at[sy, part], mright.at[sy, pl.ds(n * W, W)], table_sem.at[sy, n]))
        for n, part in enumerate((0, 0, 1)):
            for bx in range(2):
                for by in range(2):
                    tables.append(pltpu.make_async_copy(
                        matrices.at[sy, part, pl.ds(by * HALF, HALF), pl.ds(bx * HALF, HALF)],
                        mleft.at[sy, pl.ds(bx * HALF, HALF), pl.ds(n * W + by * HALF, HALF)],
                        table_sem.at[sy, 3 + n * 4 + bx * 2 + by]))
    for copy in tables:
        copy.start()
    grid[...] = lax.broadcasted_iota(jnp.int32, (W, W), 0).astype(f32).astype(bf16)

    def build(r, carry):
        spline_rows(tx, r, grid, gcells[r, 0:1, :], gshifts[r, 0:1, :])
        spline_rows(ty, r, grid, gcells[r, 1:2, :], gshifts[r, 1:2, :])
        return carry

    gcells[0:CHAINS] = cells[...]
    gshifts[0:CHAINS] = shifts[...]
    lax.fori_loop(0, CHAINS, build, 0)
    load.wait()
    for copy in tables:
        copy.wait()

    def advance(u, base, theta):
        sine, cosine = sincos(theta)
        for k in range(2):
            r = base + k + met[u]
            c, s = cosine[k : k + 1].astype(bf16), -sine[k : k + 1].astype(bf16)
            for row in range(0, W, 64):
                weights = tx[r, row : row + 64, :]
                dep[k, row : row + 64, :] = weights * c
                dep[k, W + row : W + row + 64, :] = weights * s
            cur[k] = lax.dot_general(dep[k], ty[r], (((1,), (1,)), ((), ())), preferred_element_type=f32)
        for k in range(2):
            chain = base + k
            at = me * CHAINS + chain
            keep = 1.0
            if u:
                keep = jnp.where((at + met[u] >= NS) & (at + met[u - 1] < NS), 0.0, 1.0)
            for c in range(2):
                for row in range(0, HALF, 32):
                    top = field[chain, c, row : row + 32, :] * keep + GAIN * cur[k, c * W + row : c * W + row + 32, :]
                    low = row + HALF
                    bottom = field[chain, c, low : low + 32, :] * keep + GAIN * cur[k, c * W + low : c * W + low + 32, :]
                    for sx, v in enumerate((top + bottom, top - bottom)):
                        a, b = v[:, :HALF], v[:, HALF:]
                        rows = slice(sx * HALF + row, sx * HALF + row + 32)
                        for sy, g in enumerate((a + b, a - b)):
                            hi, lo = split(g)
                            lhs[k, sy, rows, c * HALF : c * HALF + HALF] = hi
                            lhs[k, sy, rows, W + c * HALF : W + c * HALF + HALF] = hi
                            lhs[k, sy, rows, 2 * W + c * HALF : 2 * W + c * HALF + HALF] = lo
            for sy in range(2):
                mid = jnp.dot(lhs[k, sy], mright[sy], preferred_element_type=f32)
                for sx in range(2):
                    for c in range(2):
                        hi, lo = split(mid[sx * HALF : sx * HALF + HALF, c * HALF : c * HALF + HALF])
                        cols = slice(sy * HALF, sy * HALF + HALF)
                        rhs[k, sx, c * HALF : c * HALF + HALF, cols] = hi
                        rhs[k, sx, W + c * HALF : W + c * HALF + HALF, cols] = lo
                        rhs[k, sx, 2 * W + c * HALF : 2 * W + c * HALF + HALF, cols] = hi
        for k in range(2):
            chain = base + k
            at = me * CHAINS + chain
            za = jnp.dot(mleft[0], rhs[k, 0], preferred_element_type=f32)
            zb = jnp.dot(mleft[1], rhs[k, 1], preferred_element_type=f32)
            for c in range(2):
                p, n = za[c * HALF : c * HALF + HALF], zb[c * HALF : c * HALF + HALF]
                for hx, v in enumerate((p + n, p - n)):
                    a, b = v[:, :HALF], v[:, HALF:]
                    for hy, g in enumerate((a + b, a - b)):
                        cols = slice(hy * HALF, hy * HALF + HALF)
                        rounded[chain, c * W + hx * HALF : c * W + hx * HALF + HALF, cols] = g.astype(bf16)
                        if u < STEPS - 1:
                            field[chain, c, hx * HALF : hx * HALF + HALF, cols] = g
                        else:
                            gone = (at + met[STEPS] >= NS) & (at + met[STEPS - 1] < NS)
                            row = (2 * hx + hy) * 8 + c * CHAINS + chain
                            sent[pl.ds(row, HALF, stride=32), :] = g * jnp.where(gone, 0.0, 1.0)
        return sine, cosine

    def push(u, base, theta, eta, sine, cosine):
        sampled = []
        for k in range(2):
            r = base + k + met[u]
            pieces = []
            for q in range(0, P_SIZE, 256):
                picked = jnp.dot(rounded[base + k], ty[r, :, q : q + 256], preferred_element_type=f32)
                weights = tx[r, :, q : q + 256].astype(f32)
                pieces.append([jnp.sum(picked[c * W : c * W + W] * weights, axis=0, keepdims=True) for c in range(2)])
            sampled.append([jnp.concatenate([piece[c] for piece in pieces], axis=1) for c in range(2)])
        first = jnp.concatenate([sampled[0][0], sampled[1][0]], axis=0)
        second = jnp.concatenate([sampled[0][1], sampled[1][1]], axis=0)
        eta = eta - 0.5 * (first * cosine - second * sine)
        state[u, 0, base : base + 2, :] = theta + eta
        state[u, 1, base : base + 2, :] = eta

    def exchange(u):
        return [
            pltpu.make_async_remote_copy(
                state.at[u, n, pl.ds(0, 2)], arrived.at[u, n], ps.at[u, n], pr.at[u, n],
                device_id=place(me - 1), device_id_type=MESH)
            for n in range(2)
        ]

    geometry = []
    for n, (src, dst) in enumerate(((cells, gcells), (shifts, gshifts))):
        geometry.append(pltpu.make_async_remote_copy(
            src, dst.at[pl.ds(4, 4)], gs.at[n], gr.at[n], device_id=place(me - 1), device_id_type=MESH))
        geometry.append(pltpu.make_async_remote_copy(
            src.at[pl.ds(0, 2)], dst.at[pl.ds(8, 2)], gs.at[n + 2], gr.at[n + 2],
            device_id=place(me - 2), device_id_type=MESH))

    def front(u):
        if not u:
            return phases[0:2], energy[0:2]
        one = slips[u - 1] == 1
        return [jnp.where(one, state[u - 1, n, 1:3, :], state[u - 1, n, 2:4, :]) for n in range(2)]

    def rear(u):
        if not u:
            return phases[2:4], energy[2:4]
        one = slips[u - 1] == 1
        return [
            jnp.where(
                one,
                jnp.concatenate([state[u - 1, n, 3:4, :], arrived[u - 1, n, 0:1, :]], axis=0),
                arrived[u - 1, n],
            )
            for n in range(2)
        ]

    moving = []
    for u in range(STEPS - 1):
        theta, eta = front(u)
        push(u, 0, theta, eta, *advance(u, 0, theta))
        if u == 0:
            pl.semaphore_wait(barrier, DEVICES - 1)
            for copy in geometry:
                copy.start()
        for copy in moving:
            copy.wait()
        if u == 1:
            for copy in geometry:
                copy.wait()
            lax.fori_loop(CHAINS, REACH, build, 0)
        moving = exchange(u)
        for copy in moving:
            copy.start()
        theta, eta = rear(u)
        push(u, 2, theta, eta, *advance(u, 2, theta))
    last = STEPS - 1
    ahead = front(last)
    ahead_turn = advance(last, 0, ahead[0])
    for copy in moving:
        copy.wait()
    behind = rear(last)
    behind_turn = advance(last, 2, behind[0])

    def spread(src, dst, q, ss, rs):
        for there in others:
            n = there[0] * FINE + there[1]
            pltpu.make_async_remote_copy(
                src.at[pl.ds(n * 32 + q * ROWS, ROWS)], dst.at[pl.ds(me * 32 + q * ROWS, ROWS)], ss.at[q], rs.at[q],
                device_id=there, device_id_type=MESH).start()

    def settle(ref, q, sem):
        view = ref.at[pl.ds(0, (DEVICES - 1) * ROWS)]
        pltpu.make_async_copy(view, view, sem.at[q]).wait()

    for q in range(PARTS):
        spread(sent, got, q, s1, r1)
    mine = pl.ds(pl.multiple_of(me * 32, 32), 32)
    got[mine, :] = sent[mine, :]
    push(last, 0, *ahead, *ahead_turn)
    push(last, 2, *behind, *behind_turn)
    homing = [
        pltpu.make_async_remote_copy(
            state.at[last], homes.at[n], hs.at[n], hr.at[n], device_id=place(me + n + 1), device_id_type=MESH)
        for n in range(2)
    ]
    for copy in homing:
        copy.start()

    half = NS // 2
    k = lax.broadcasted_iota(jnp.int32, (1, NS), 1)
    unit = 2.0 * np.pi / NS
    turn_quad, turn_real = sincos(((k * met[STEPS]) & (NS - 1)).astype(f32) * unit)
    br, bi = bragg[0:1, :] * (1.0 / NS), bragg[1:2, :] * (1.0 / NS)
    response = jnp.concatenate([br * turn_real + bi * turn_quad, bi * turn_real - br * turn_quad], axis=0)
    hi, rest = response.astype(bf16), None
    rest = response - hi.astype(f32)
    lo = rest.astype(bf16)
    tiny = (rest - lo.astype(f32)).astype(bf16)
    down = lax.broadcasted_iota(jnp.int32, (NS, NS), 0)
    across = lax.broadcasted_iota(jnp.int32, (NS, NS), 1)
    picks = jnp.where(down == ((2 * across) & (NS - 1)) + (across >> 8), 1.0, 0.0).astype(bf16)
    ordered = (
        jnp.dot(hi, picks, preferred_element_type=f32)
        + jnp.dot(lo, picks, preferred_element_type=f32)
        + jnp.dot(tiny, picks, preferred_element_type=f32)
    )
    for parity in range(2):
        real = ordered[0:1, parity * half : parity * half + half]
        quad = ordered[1:2, parity * half : parity * half + half]

        def fill(block, carry, parity=parity, real=real, quad=quad):
            start = pl.multiple_of(block * 32, 32)
            row = lax.broadcasted_iota(jnp.int32, (32, half), 0) + start
            m = lax.broadcasted_iota(jnp.int32, (32, half), 1)
            time = (row >> 3) * 4 + (row & 3)
            upper = (row & 4) == 0
            s, c = sincos((((2 * m + parity) * time) & (NS - 1)).astype(f32) * unit)
            wr = jnp.where(upper, c, s)
            wi = jnp.where(upper, -s, c)
            for n, (w, g) in enumerate(((wr, wr * real + wi * quad), (wi, wi * real - wr * quad))):
                cols = slice(n * half, n * half + half)
                hi, lo = split(w)
                wave[0, pl.ds(start, 32), cols] = hi
                wave[1, pl.ds(start, 32), cols] = lo
                hi, lo = split(g)
                turned[0, pl.ds(start, 32), cols] = hi
                turned[1, pl.ds(start, 32), cols] = lo
            return carry

        lax.fori_loop(0, NS // 32, fill, 0)
        dims = (((1,), (1,)), ((), ()))
        for row in range(0, NS, 256):
            rows = slice(row, row + 256)
            kernel = (
                lax.dot_general(turned[0, rows], wave[0], dims, preferred_element_type=f32)
                + lax.dot_general(turned[0, rows], wave[1], dims, preferred_element_type=f32)
                + lax.dot_general(turned[1, rows], wave[0], dims, preferred_element_type=f32)
            )
            hi, lo = split(kernel)
            conv[parity, rows, 0:NS] = hi
            conv[parity, rows, NS : 2 * NS] = hi
            conv[parity, rows, 2 * NS : 3 * NS] = lo

    mid = DEVICES // 2
    tiles = 4 // PARTS
    for q in range(PARTS):
        settle(got, q, r1)
        for tile in range(tiles):
            lanes = slice(tile * HALF, tile * HALF + HALF)
            for block in range(0, mid, 8):
                rows = block * 8
                pieces = []
                for start in (block, mid + block):
                    pieces.append(jnp.concatenate(
                        [got[(start + n) * 32 + (q * tiles + tile) * 8 : (start + n) * 32 + (q * tiles + tile) * 8 + 8, :] for n in range(8)],
                        axis=0))
                a, b = pieces
                for parity, g in enumerate((a + b, a - b)):
                    hi, lo = split(g)
                    operand[parity, rows : rows + 64, lanes] = hi
                    operand[parity, NS + rows : NS + rows + 64, lanes] = lo
                    operand[parity, 2 * NS + rows : 2 * NS + rows + 64, lanes] = hi
        for block in range(0, NS, 256):
            even = jnp.dot(conv[0, block : block + 256, :], operand[0], preferred_element_type=f32)
            odd = jnp.dot(conv[1, block : block + 256, :], operand[1], preferred_element_type=f32)
            total, gap = even + odd, even - odd
            for tile in range(tiles):
                lanes = slice(tile * HALF, tile * HALF + HALF)
                for n in range(32):
                    to = (block // 8 + n) * 32 + (q * tiles + tile) * 8
                    result[to : to + 8, :] = total[n * 8 : n * 8 + 8, lanes]
                    result[mid * 32 + to : mid * 32 + to + 8, :] = gap[n * 8 : n * 8 + 8, lanes]
        spread(result, back, q, s2, r2)
    own = pltpu.make_async_copy(result.at[mine], back.at[mine], own_sem)
    own.start()
    for copy in homing:
        copy.wait()
    for i in range(CHAINS):
        at = i - met[last]
        for n in range(2):
            value = homes[1, n, pl.ds(jnp.clip(at + 8, 0, 3), 1), :]
            value = jnp.where(at >= -4, homes[0, n, pl.ds(jnp.clip(at + 4, 0, 3), 1), :], value)
            value = jnp.where(at >= 0, state[last, n, pl.ds(jnp.clip(at, 0, 3), 1), :], value)
            particles[i, n : n + 1, :] = value
    own.wait()
    for q in range(PARTS):
        settle(got, q, s1)
        settle(got, q, s2)
        settle(got, q, r2)


def unblock_kernel(blocks, out, staged, sems):
    copies = []
    for chain in range(CHAINS):
        for c in range(2):
            for hx in range(2):
                for hy in range(2):
                    staged[chain, c, hx * HALF : hx * HALF + HALF, hy * HALF : hy * HALF + HALF] = blocks[
                        pl.ds((2 * hx + hy) * 8 + c * CHAINS + chain, HALF, stride=32), :
                    ]
        copy = pltpu.make_async_copy(staged.at[chain], out.at[chain], sems.at[chain])
        copy.start()
        copies.append(copy)
    for copy in copies:
        copy.wait()


def on_device(field_in, phases, energy, cell_index, offsets, slip_plan, bragg_response):
    vmem = pl.BlockSpec(memory_space=pltpu.VMEM)
    smem = pl.BlockSpec(memory_space=pltpu.SMEM)
    whole = pl.BlockSpec(memory_space=pl.ANY)
    dma = pltpu.SemaphoreType.DMA
    back, particles = pl.pallas_call(
        whole_kernel,
        out_shape=(
            jax.ShapeDtypeStruct((DEVICES * 32, HALF), f32),
            jax.ShapeDtypeStruct((CHAINS, 2, P_SIZE), f32),
        ),
        in_specs=[smem, whole, vmem, vmem, vmem, vmem, vmem, whole],
        out_specs=(whole, vmem),
        scratch_shapes=[
            pltpu.VMEM((CHAINS, 2, W, W), f32),
            pltpu.VMEM((REACH, W, P_SIZE), bf16),
            pltpu.VMEM((REACH, W, P_SIZE), bf16),
            pltpu.VMEM((W, W), bf16),
            pltpu.VMEM((REACH, 2, P_SIZE), jnp.int32),
            pltpu.VMEM((REACH, 2, P_SIZE), f32),
            pltpu.VMEM((STEPS, 2, CHAINS, P_SIZE), f32),
            pltpu.VMEM((STEPS, 2, 2, P_SIZE), f32),
            pltpu.VMEM((2, 2 * W, P_SIZE), bf16),
            pltpu.VMEM((2, 2 * W, W), f32),
            pltpu.VMEM((2, 3 * W, W), bf16),
            pltpu.VMEM((2, W, 3 * W), bf16),
            pltpu.VMEM((2, 2, W, 3 * W), bf16),
            pltpu.VMEM((2, 2, 3 * W, W), bf16),
            pltpu.VMEM((CHAINS, 2 * W, W), bf16),
            pltpu.VMEM((DEVICES * 32, HALF), f32),
            pltpu.VMEM((DEVICES * 32, HALF), f32),
            pltpu.VMEM((DEVICES * 32, HALF), f32),
            pltpu.VMEM((2, NS, NS), bf16),
            pltpu.VMEM((2, NS, NS), bf16),
            pltpu.VMEM((2, NS, 3 * NS), bf16),
            pltpu.VMEM((2, 3 * NS, 2 * W // PARTS), bf16),
            pltpu.VMEM((2, 2, CHAINS, P_SIZE), f32),
            dma,
            dma((2, 15)),
            dma((4,)),
            dma((4,)),
            dma((STEPS, 2)),
            dma((STEPS, 2)),
            dma,
            dma((PARTS,)),
            dma((PARTS,)),
            dma((PARTS,)),
            dma((PARTS,)),
            dma((2,)),
            dma((2,)),
        ],
        compiler_params=pltpu.CompilerParams(
            collective_id=0, has_side_effects=True, vmem_limit_bytes=52 << 20
        ),
        name="pass",
    )(slip_plan, field_in, phases, energy, cell_index, offsets, bragg_response, jnp.asarray(diffraction_tables()))
    field_out = pl.pallas_call(
        unblock_kernel,
        out_shape=jax.ShapeDtypeStruct((CHAINS, 2, W, W), f32),
        in_specs=[vmem],
        out_specs=whole,
        scratch_shapes=[pltpu.VMEM((CHAINS, 2, W, W), f32), dma((CHAINS,))],
        compiler_params=pltpu.CompilerParams(vmem_limit_bytes=8 << 20),
        name="unblock",
    )(back)
    return field_out, particles


def solution(mesh):
    axes = ("coarse", "fine")
    in_specs = (
        P(axes, None, None, None),
        P(axes, None),
        P(axes, None),
        P(axes, None, None),
        P(axes, None, None),
        P(),
        P(),
    )
    out_specs = (P(axes, None, None, None), P(axes, None, None))
    return jax.shard_map(on_device, mesh=mesh, in_specs=in_specs, out_specs=out_specs, check_vma=False)
```

```python
import itertools

import jax
import jax.numpy as jnp
import numpy as np
from jax import lax
from jax.experimental import pallas as pl
from jax.experimental.pallas import tpu as pltpu
from jax.sharding import PartitionSpec as P

W = 256
HALF = 128
P_SIZE = 1024
STEPS = 4
NS = 512
CHAINS = 4
COARSE = 8
FINE = 16
DEVICES = COARSE * FINE
REACH = 10
GAIN = 0.25 * W * W / P_SIZE
SPREAD = 20.0
VMEM_ALL = 67043328
MESH = pl.DeviceIdType.MESH
f32, bf16 = jnp.float32, jnp.bfloat16


def halves(matrix):
    high = matrix.astype(np.float32).astype(bf16)
    low = (matrix - high.astype(np.float64)).astype(np.float32).astype(bf16)
    return high, low


def diffraction_tables():
    k = np.arange(W)
    signed = np.where(k < W // 2, k, k - W)
    h = np.exp(-1j * SPREAD * (2.0 * np.pi * signed / W) ** 2)
    q = np.fft.ifft(h)
    full = q[(k[:, None] - k[None, :]) % W]
    a, b = full[:HALF, :HALF], full[:HALF, HALF:]
    tables = []
    for part in (0.5 * (a + b), 0.5 * (a - b)):
        t = part.T
        tables.append(np.stack(halves(np.block([[t.real, t.imag], [-t.imag, t.real]]))))
    return np.stack(tables)


def place(n):
    n = lax.rem(n + 2 * DEVICES, DEVICES)
    return (n // FINE, lax.rem(n, FINE))


def far_first():
    offsets = [o for o in itertools.product(range(4), range(4), range(4), range(2)) if any(o)]
    mixed = np.random.RandomState(1).permutation(len(offsets))
    offsets = [offsets[i] for i in mixed]
    return sorted(offsets, key=lambda o: -sum(min(v, 4 - v) for v in o[:3]))


def partners():
    coarse, fine = lax.axis_index("coarse"), lax.axis_index("fine")
    x, y = fine // 4, coarse // 2
    z, core = (lax.rem(fine, 4) // 2) * 2 + lax.rem(coarse, 2), lax.rem(fine, 2)
    out = []
    for dx, dy, dz, dk in far_first():
        px, py, pz, pk = lax.rem(x + dx, 4), lax.rem(y + dy, 4), lax.rem(z + dz, 4), lax.rem(core + dk, 2)
        out.append((py * 2 + lax.rem(pz, 2), px * 4 + (pz // 2) * 2 + pk))
    return out


def sincos(x):
    turns = jnp.round(x * (2.0 / np.pi))
    r = x - turns * 1.5703125
    r = r - turns * 4.837512969970703125e-4
    r = r - turns * 7.54978995489188216e-8
    z = r * r
    sine = r + r * z * (-1.6666654611e-1 + z * (8.3321608736e-3 + z * -1.9515295891e-4))
    cosine = 1.0 - 0.5 * z + z * z * (4.166664568298827e-2 + z * (-1.388731625493765e-3 + z * 2.443315711809948e-5))
    quadrant = turns.astype(jnp.int32) & 3
    odd = (quadrant & 1) == 1
    s = jnp.where(odd, cosine, sine)
    c = jnp.where(odd, sine, cosine)
    s = jnp.where(quadrant >= 2, -s, s)
    c = jnp.where((quadrant == 1) | (quadrant == 2), -c, c)
    return s, c


def spline_rows(table, r, grid, cells, shifts):
    left = (0.5 * (0.5 - shifts) * (0.5 - shifts)).astype(bf16)
    middle = (0.75 - shifts * shifts).astype(bf16)
    right = (0.5 * (0.5 + shifts) * (0.5 + shifts)).astype(bf16)
    before = ((cells - 1) & (W - 1)).astype(f32).astype(bf16)
    after = ((cells + 1) & (W - 1)).astype(f32).astype(bf16)
    at = cells.astype(f32).astype(bf16)
    none = jnp.zeros((), bf16)
    for q in range(0, P_SIZE, W):
        lanes = slice(q, q + W)
        for row in range(0, W, 64):
            rows = grid[row : row + 64, :]
            value = jnp.where(rows == before[:, lanes], left[:, lanes], none)
            value = jnp.where(rows == at[:, lanes], middle[:, lanes], value)
            value = jnp.where(rows == after[:, lanes], right[:, lanes], value)
            table[r, row : row + 64, lanes] = value


def split(g):
    hi = g.astype(bf16)
    return hi, (g - hi.astype(f32)).astype(bf16)


def whole_kernel(
    plan, field_in, phases_in, energy_in, cells_in, shifts_in, bragg_in, matrices, back, particles,
    phases, energy, cells, shifts, bragg, field, tx, ty, grid, gcells, gshifts, state, arrived, dep, cur, mright, mleft, lhs, rhs, rounded,
    sent, got, result, wave, turned, conv, operand, homes,
    small_sem, field_sem, table_sem, gs, gr, ps, pr, own_sem, s1, r1, s2, r2, hs, hr,
):
    coarse, fine = lax.axis_index("coarse"), lax.axis_index("fine")
    me = coarse * FINE + fine
    others = partners()
    slips = [plan[u] for u in range(STEPS)]
    met = [0]
    for u in range(STEPS):
        met.append(met[u] + slips[u])

    small = [
        pltpu.make_async_copy(src, dst, small_sem.at[n])
        for n, (src, dst) in enumerate((
            (cells_in, cells), (shifts_in, shifts), (phases_in, phases), (energy_in, energy), (bragg_in, bragg)))
    ]
    for copy in small:
        copy.start()
    load = pltpu.make_async_copy(field_in, field, field_sem)
    load.start()
    tables = []
    for sy in range(2):
        for n, part in enumerate((0, 1, 0)):
            tables.append(pltpu.make_async_copy(
                matrices.at[sy, part], mright.at[sy, pl.ds(n * W, W)], table_sem.at[sy, n]))
        for n, part in enumerate((0, 0, 1)):
            for bx in range(2):
                for by in range(2):
                    tables.append(pltpu.make_async_copy(
                        matrices.at[sy, part, pl.ds(by * HALF, HALF), pl.ds(bx * HALF, HALF)],
                        mleft.at[sy, pl.ds(bx * HALF, HALF), pl.ds(n * W + by * HALF, HALF)],
                        table_sem.at[sy, 3 + n * 4 + bx * 2 + by]))
    for copy in tables:
        copy.start()
    barrier = pltpu.get_barrier_semaphore()
    for there in others:
        pl.semaphore_signal(barrier, inc=1, device_id=there, device_id_type=MESH)
    grid[...] = lax.broadcasted_iota(jnp.int32, (W, W), 0).astype(f32).astype(bf16)

    def build(r, carry):
        spline_rows(tx, r, grid, gcells[r, 0:1, :], gshifts[r, 0:1, :])
        spline_rows(ty, r, grid, gcells[r, 1:2, :], gshifts[r, 1:2, :])
        return carry

    for copy in small:
        copy.wait()
    gcells[0:CHAINS] = cells[...]
    gshifts[0:CHAINS] = shifts[...]
    lax.fori_loop(0, CHAINS, build, 0)
    load.wait()
    for copy in tables:
        copy.wait()

    def advance(u, base, theta):
        sine, cosine = sincos(theta)
        for k in range(2):
            r = base + k + met[u]
            c, s = cosine[k : k + 1].astype(bf16), -sine[k : k + 1].astype(bf16)
            for row in range(0, W, 64):
                weights = tx[r, row : row + 64, :]
                dep[k, row : row + 64, :] = weights * c
                dep[k, W + row : W + row + 64, :] = weights * s
            cur[k] = lax.dot_general(dep[k], ty[r], (((1,), (1,)), ((), ())), preferred_element_type=f32)
        for k in range(2):
            chain = base + k
            at = me * CHAINS + chain
            keep = 1.0
            if u:
                keep = jnp.where((at + met[u] >= NS) & (at + met[u - 1] < NS), 0.0, 1.0)
            for c in range(2):
                for row in range(0, HALF, 32):
                    top = field[chain, c, row : row + 32, :] * keep + GAIN * cur[k, c * W + row : c * W + row + 32, :]
                    low = row + HALF
                    bottom = field[chain, c, low : low + 32, :] * keep + GAIN * cur[k, c * W + low : c * W + low + 32, :]
                    for sx, v in enumerate((top + bottom, top - bottom)):
                        a, b = v[:, :HALF], v[:, HALF:]
                        rows = slice(sx * HALF + row, sx * HALF + row + 32)
                        for sy, g in enumerate((a + b, a - b)):
                            hi, lo = split(g)
                            lhs[k, sy, rows, c * HALF : c * HALF + HALF] = hi
                            lhs[k, sy, rows, W + c * HALF : W + c * HALF + HALF] = hi
                            lhs[k, sy, rows, 2 * W + c * HALF : 2 * W + c * HALF + HALF] = lo
            for sy in range(2):
                mid = jnp.dot(lhs[k, sy], mright[sy], preferred_element_type=f32)
                for sx in range(2):
                    for c in range(2):
                        hi, lo = split(mid[sx * HALF : sx * HALF + HALF, c * HALF : c * HALF + HALF])
                        cols = slice(sy * HALF, sy * HALF + HALF)
                        rhs[k, sx, c * HALF : c * HALF + HALF, cols] = hi
                        rhs[k, sx, W + c * HALF : W + c * HALF + HALF, cols] = lo
                        rhs[k, sx, 2 * W + c * HALF : 2 * W + c * HALF + HALF, cols] = hi
        for k in range(2):
            chain = base + k
            at = me * CHAINS + chain
            za = jnp.dot(mleft[0], rhs[k, 0], preferred_element_type=f32)
            zb = jnp.dot(mleft[1], rhs[k, 1], preferred_element_type=f32)
            for c in range(2):
                p, n = za[c * HALF : c * HALF + HALF], zb[c * HALF : c * HALF + HALF]
                for hx, v in enumerate((p + n, p - n)):
                    a, b = v[:, :HALF], v[:, HALF:]
                    for hy, g in enumerate((a + b, a - b)):
                        cols = slice(hy * HALF, hy * HALF + HALF)
                        rounded[chain, c * W + hx * HALF : c * W + hx * HALF + HALF, cols] = g.astype(bf16)
                        if u < STEPS - 1:
                            field[chain, c, hx * HALF : hx * HALF + HALF, cols] = g
                        else:
                            gone = (at + met[STEPS] >= NS) & (at + met[STEPS - 1] < NS)
                            sent[base + hy, pl.ds(hx * 4 + c * 2 + k, HALF, stride=8), :] = g * jnp.where(gone, 0.0, 1.0)
        return sine, cosine

    def push(u, base, theta, eta, sine, cosine):
        sampled = []
        for k in range(2):
            r = base + k + met[u]
            pieces = []
            for q in range(0, P_SIZE, 256):
                picked = jnp.dot(rounded[base + k], ty[r, :, q : q + 256], preferred_element_type=f32)
                weights = tx[r, :, q : q + 256].astype(f32)
                pieces.append([jnp.sum(picked[c * W : c * W + W] * weights, axis=0, keepdims=True) for c in range(2)])
            sampled.append([jnp.concatenate([piece[c] for piece in pieces], axis=1) for c in range(2)])
        first = jnp.concatenate([sampled[0][0], sampled[1][0]], axis=0)
        second = jnp.concatenate([sampled[0][1], sampled[1][1]], axis=0)
        eta = eta - 0.5 * (first * cosine - second * sine)
        state[u, 0, base : base + 2, :] = theta + eta
        state[u, 1, base : base + 2, :] = eta

    def exchange(u):
        return [
            pltpu.make_async_remote_copy(
                state.at[u, n, pl.ds(0, 2)], arrived.at[u, n], ps.at[u, n], pr.at[u, n],
                device_id=place(me - 1), device_id_type=MESH)
            for n in range(2)
        ]

    geometry = []
    for n, (src, dst) in enumerate(((cells, gcells), (shifts, gshifts))):
        geometry.append(pltpu.make_async_remote_copy(
            src, dst.at[pl.ds(4, 4)], gs.at[n], gr.at[n], device_id=place(me - 1), device_id_type=MESH))
        geometry.append(pltpu.make_async_remote_copy(
            src.at[pl.ds(0, 2)], dst.at[pl.ds(8, 2)], gs.at[n + 2], gr.at[n + 2],
            device_id=place(me - 2), device_id_type=MESH))

    def front(u):
        if not u:
            return phases[0:2], energy[0:2]
        one = slips[u - 1] == 1
        return [jnp.where(one, state[u - 1, n, 1:3, :], state[u - 1, n, 2:4, :]) for n in range(2)]

    def rear(u):
        if not u:
            return phases[2:4], energy[2:4]
        one = slips[u - 1] == 1
        return [
            jnp.where(
                one,
                jnp.concatenate([state[u - 1, n, 3:4, :], arrived[u - 1, n, 0:1, :]], axis=0),
                arrived[u - 1, n],
            )
            for n in range(2)
        ]

    moving = []
    for u in range(STEPS - 1):
        theta, eta = front(u)
        push(u, 0, theta, eta, *advance(u, 0, theta))
        if u == 0:
            pl.semaphore_wait(barrier, DEVICES - 1)
            for copy in geometry:
                copy.start()
        for copy in moving:
            copy.wait()
        if u == 1:
            for copy in geometry:
                copy.wait()
            lax.fori_loop(CHAINS, REACH, build, 0)
        moving = exchange(u)
        for copy in moving:
            copy.start()
        theta, eta = rear(u)
        push(u, 2, theta, eta, *advance(u, 2, theta))
    last = STEPS - 1
    def spread(src, dst, first, count, ss, rs):
        parts = pl.ds(first, count)
        for there in others:
            n = there[0] * FINE + there[1]
            pltpu.make_async_remote_copy(
                src.at[parts, pl.ds(n * 8, 8)], dst.at[parts, pl.ds(me * 8, 8)], ss, rs,
                device_id=there, device_id_type=MESH).start()

    def settle(ref, count, sem):
        view = ref.at[pl.ds(0, count), pl.ds(0, (DEVICES - 1) * 8)]
        pltpu.make_async_copy(view, view, sem).wait()

    ahead = front(last)
    ahead_turn = advance(last, 0, ahead[0])
    spread(sent, got, 0, 2, s1.at[0], r1.at[0])
    for copy in moving:
        copy.wait()
    behind = rear(last)
    behind_turn = advance(last, 2, behind[0])
    spread(sent, got, 2, 1, s1.at[1], r1.at[1])
    spread(sent, got, 3, 1, s1.at[2], r1.at[2])
    mine = pl.ds(pl.multiple_of(me * 8, 8), 8)
    for part in range(4):
        got[part, mine, :] = sent[part, mine, :]
    push(last, 0, *ahead, *ahead_turn)
    push(last, 2, *behind, *behind_turn)
    homing = [
        pltpu.make_async_remote_copy(
            state.at[last], homes.at[n], hs.at[n], hr.at[n], device_id=place(me + n + 1), device_id_type=MESH)
        for n in range(2)
    ]
    for copy in homing:
        copy.start()

    half = NS // 2
    k = lax.broadcasted_iota(jnp.int32, (1, NS), 1)
    unit = 2.0 * np.pi / NS
    turn_quad, turn_real = sincos(((k * met[STEPS]) & (NS - 1)).astype(f32) * unit)
    br, bi = bragg[0:1, :] * (1.0 / NS), bragg[1:2, :] * (1.0 / NS)
    response = jnp.concatenate([br * turn_real + bi * turn_quad, bi * turn_real - br * turn_quad], axis=0)
    hi, rest = response.astype(bf16), None
    rest = response - hi.astype(f32)
    lo = rest.astype(bf16)
    tiny = (rest - lo.astype(f32)).astype(bf16)
    down = lax.broadcasted_iota(jnp.int32, (NS, NS), 0)
    across = lax.broadcasted_iota(jnp.int32, (NS, NS), 1)
    picks = jnp.where(down == ((2 * across) & (NS - 1)) + (across >> 8), 1.0, 0.0).astype(bf16)
    ordered = (
        jnp.dot(hi, picks, preferred_element_type=f32)
        + jnp.dot(lo, picks, preferred_element_type=f32)
        + jnp.dot(tiny, picks, preferred_element_type=f32)
    )
    for parity in range(2):
        real = ordered[0:1, parity * half : parity * half + half]
        quad = ordered[1:2, parity * half : parity * half + half]

        def fill(block, carry, parity=parity, real=real, quad=quad):
            start = pl.multiple_of(block * 32, 32)
            row = lax.broadcasted_iota(jnp.int32, (32, half), 0) + start
            m = lax.broadcasted_iota(jnp.int32, (32, half), 1)
            time = (row >> 3) * 4 + ((row >> 2) & 1) * 2 + (row & 1)
            upper = (row & 2) == 0
            s, c = sincos((((2 * m + parity) * time) & (NS - 1)).astype(f32) * unit)
            wr = jnp.where(upper, c, s)
            wi = jnp.where(upper, -s, c)
            for n, (w, g) in enumerate(((wr, wr * real + wi * quad), (wi, wi * real - wr * quad))):
                cols = slice(n * half, n * half + half)
                hi, lo = split(w)
                wave[0, pl.ds(start, 32), cols] = hi
                wave[1, pl.ds(start, 32), cols] = lo
                hi, lo = split(g)
                turned[0, pl.ds(start, 32), cols] = hi
                turned[1, pl.ds(start, 32), cols] = lo
            return carry

        lax.fori_loop(0, NS // 32, fill, 0)
        dims = (((1,), (1,)), ((), ()))
        for row in range(0, NS, 256):
            rows = slice(row, row + 256)
            kernel = (
                lax.dot_general(turned[0, rows], wave[0], dims, preferred_element_type=f32)
                + lax.dot_general(turned[0, rows], wave[1], dims, preferred_element_type=f32)
                + lax.dot_general(turned[1, rows], wave[0], dims, preferred_element_type=f32)
            )
            hi, lo = split(kernel)
            conv[parity, rows, 0:NS] = hi
            conv[parity, rows, NS : 2 * NS] = hi
            conv[parity, rows, 2 * NS : 3 * NS] = lo

    mid = DEVICES // 2
    low = lax.broadcasted_iota(jnp.int32, (8, 8, HALF), 1) < 4
    settle(got, 2, r1.at[0])
    for hy in range(2):
        settle(got, 1, r1.at[1 + hy])
        for block in range(0, mid, 8):
            pieces = []
            for start in (block, mid + block):
                a = got[hy, start * 8 : start * 8 + 64, :].reshape(8, 8, HALF)
                b = got[2 + hy, start * 8 : start * 8 + 64, :].reshape(8, 8, HALF)
                pieces.append((
                    jnp.where(low, a, pltpu.roll(b, 4, 1)).reshape(64, HALF),
                    jnp.where(low, pltpu.roll(a, 4, 1), b).reshape(64, HALF),
                ))
            for hx in range(2):
                a, b = pieces[0][hx], pieces[1][hx]
                lanes = slice(hx * HALF, hx * HALF + HALF)
                rows = block * 8
                for parity, g in enumerate((a + b, a - b)):
                    hi, lo = split(g)
                    operand[parity, rows : rows + 64, lanes] = hi
                    operand[parity, NS + rows : NS + rows + 64, lanes] = lo
                    operand[parity, 2 * NS + rows : 2 * NS + rows + 64, lanes] = hi
        for row in range(0, NS, 256):
            even = jnp.dot(conv[0, row : row + 256, :], operand[0], preferred_element_type=f32)
            odd = jnp.dot(conv[1, row : row + 256, :], operand[1], preferred_element_type=f32)
            for hx in range(2):
                a, b = even[:, hx * HALF : hx * HALF + HALF], odd[:, hx * HALF : hx * HALF + HALF]
                result[2 * hy + hx, row : row + 256, :] = a + b
                result[2 * hy + hx, mid * 8 + row : mid * 8 + row + 256, :] = a - b
        spread(result, back, 2 * hy, 2, s2.at[hy], r2.at[hy])
    own = pltpu.make_async_copy(result.at[:, mine], back.at[:, mine], own_sem)
    own.start()
    for copy in homing:
        copy.wait()
    for i in range(CHAINS):
        at = i - met[last]
        for n in range(2):
            value = homes[1, n, pl.ds(jnp.clip(at + 8, 0, 3), 1), :]
            value = jnp.where(at >= -4, homes[0, n, pl.ds(jnp.clip(at + 4, 0, 3), 1), :], value)
            value = jnp.where(at >= 0, state[last, n, pl.ds(jnp.clip(at, 0, 3), 1), :], value)
            particles[i, n : n + 1, :] = value
    own.wait()
    for n, count in enumerate((2, 1, 1)):
        settle(got, count, s1.at[n])
    for hy in range(2):
        settle(got, 2, s2.at[hy])
        settle(got, 2, r2.at[hy])


def unblock_kernel(blocks, ended, out, particles, taken, staged, kept, take_sems, put_sems, end_sems):
    near, rows = [], 2 * HALF
    for q in range(4):
        near.append(pltpu.make_async_copy(
            blocks.at[:, pl.ds(q * rows, rows)], taken.at[:, pl.ds(q * rows, rows)], take_sems.at[q]))
    ends = pltpu.make_async_copy(ended, kept, end_sems.at[0])
    for copy in near:
        copy.start()
    ends.start()
    puts = []
    for q in range(4):
        near[q].wait()
        if q == 0:
            ends.wait()
            ends = pltpu.make_async_copy(kept, particles, end_sems.at[1])
            ends.start()
        for chain in range(CHAINS):
            for c in range(2):
                row = (chain // 2) * 4 + c * 2 + chain % 2
                for hx in range(2):
                    for hy in range(2):
                        staged[chain, c, hx, q * 32 : q * 32 + 32, hy * HALF : hy * HALF + HALF] = taken[
                            2 * hy + hx, pl.ds(q * rows + row, 32, stride=8), :
                        ]
        puts.append(pltpu.make_async_copy(
            staged.at[:, :, :, pl.ds(q * 32, 32)], out.at[:, :, :, pl.ds(q * 32, 32)], put_sems.at[q]))
        puts[q].start()
    for copy in puts:
        copy.wait()
    ends.wait()


def on_device(field_in, phases, energy, cell_index, offsets, slip_plan, bragg_response):
    vmem = pl.BlockSpec(memory_space=pltpu.VMEM)
    smem = pl.BlockSpec(memory_space=pltpu.SMEM)
    whole = pl.BlockSpec(memory_space=pl.ANY)
    dma = pltpu.SemaphoreType.DMA
    far = pl.BlockSpec(memory_space=pltpu.HBM)
    back, ended = pl.pallas_call(
        whole_kernel,
        out_shape=(
            jax.ShapeDtypeStruct((4, DEVICES * 8, HALF), f32),
            jax.ShapeDtypeStruct((CHAINS, 2, P_SIZE), f32),
        ),
        in_specs=[smem] + [far] * 7,
        out_specs=(whole, vmem),
        scratch_shapes=[
            pltpu.VMEM((CHAINS, P_SIZE), f32),
            pltpu.VMEM((CHAINS, P_SIZE), f32),
            pltpu.VMEM((CHAINS, 2, P_SIZE), jnp.int32),
            pltpu.VMEM((CHAINS, 2, P_SIZE), f32),
            pltpu.VMEM((2, NS), f32),
            pltpu.VMEM((CHAINS, 2, W, W), f32),
            pltpu.VMEM((REACH, W, P_SIZE), bf16),
            pltpu.VMEM((REACH, W, P_SIZE), bf16),
            pltpu.VMEM((W, W), bf16),
            pltpu.VMEM((REACH, 2, P_SIZE), jnp.int32),
            pltpu.VMEM((REACH, 2, P_SIZE), f32),
            pltpu.VMEM((STEPS, 2, CHAINS, P_SIZE), f32),
            pltpu.VMEM((STEPS, 2, 2, P_SIZE), f32),
            pltpu.VMEM((2, 2 * W, P_SIZE), bf16),
            pltpu.VMEM((2, 2 * W, W), f32),
            pltpu.VMEM((2, 3 * W, W), bf16),
            pltpu.VMEM((2, W, 3 * W), bf16),
            pltpu.VMEM((2, 2, W, 3 * W), bf16),
            pltpu.VMEM((2, 2, 3 * W, W), bf16),
            pltpu.VMEM((CHAINS, 2 * W, W), bf16),
            pltpu.VMEM((4, DEVICES * 8, HALF), f32),
            pltpu.VMEM((4, DEVICES * 8, HALF), f32),
            pltpu.VMEM((4, DEVICES * 8, HALF), f32),
            pltpu.VMEM((2, NS, NS), bf16),
            pltpu.VMEM((2, NS, NS), bf16),
            pltpu.VMEM((2, NS, 3 * NS), bf16),
            pltpu.VMEM((2, 3 * NS, W), bf16),
            pltpu.VMEM((2, 2, CHAINS, P_SIZE), f32),
            dma((5,)),
            dma,
            dma((2, 15)),
            dma((4,)),
            dma((4,)),
            dma((STEPS, 2)),
            dma((STEPS, 2)),
            dma,
            dma((3,)),
            dma((3,)),
            dma((2,)),
            dma((2,)),
            dma((2,)),
            dma((2,)),
        ],
        compiler_params=pltpu.CompilerParams(
            collective_id=0, has_side_effects=True, vmem_limit_bytes=VMEM_ALL
        ),
        name="pass",
    )(slip_plan, field_in, phases, energy, cell_index, offsets, bragg_response, jnp.asarray(diffraction_tables()))
    field_out, particles = pl.pallas_call(
        unblock_kernel,
        out_shape=(
            jax.ShapeDtypeStruct((CHAINS, 2, 2, HALF, W), f32),
            jax.ShapeDtypeStruct((CHAINS, 2, P_SIZE), f32),
        ),
        in_specs=[far, far],
        out_specs=(far, far),
        scratch_shapes=[
            pltpu.VMEM((4, DEVICES * 8, HALF), f32),
            pltpu.VMEM((CHAINS, 2, 2, HALF, W), f32),
            pltpu.VMEM((CHAINS, 2, P_SIZE), f32),
            dma((4,)),
            dma((4,)),
            dma((2,)),
        ],
        compiler_params=pltpu.CompilerParams(vmem_limit_bytes=VMEM_ALL),
        name="unblock",
    )(back, ended)
    return field_out.reshape(CHAINS, 2, W, W), particles


def solution(mesh):
    axes = ("coarse", "fine")
    in_specs = (
        P(axes, None, None, None),
        P(axes, None),
        P(axes, None),
        P(axes, None, None),
        P(axes, None, None),
        P(),
        P(),
    )
    out_specs = (P(axes, None, None, None), P(axes, None, None))
    return jax.shard_map(on_device, mesh=mesh, in_specs=in_specs, out_specs=out_specs, check_vma=False)
```

```python
import itertools

import jax
import jax.numpy as jnp
import numpy as np
from jax import lax
from jax.experimental import pallas as pl
from jax.experimental.pallas import tpu as pltpu
from jax.sharding import PartitionSpec as P

W = 256
HALF = 128
P_SIZE = 1024
STEPS = 4
NS = 512
CHAINS = 4
COARSE = 8
FINE = 16
DEVICES = COARSE * FINE
REACH = 10
GAIN = 0.25 * W * W / P_SIZE
SPREAD = 20.0
VMEM_ALL = 67043328
MESH = pl.DeviceIdType.MESH
f32, bf16 = jnp.float32, jnp.bfloat16


def halves(matrix):
    high = matrix.astype(np.float32).astype(bf16)
    low = (matrix - high.astype(np.float64)).astype(np.float32).astype(bf16)
    return high, low


def diffraction_tables():
    k = np.arange(W)
    signed = np.where(k < W // 2, k, k - W)
    h = np.exp(-1j * SPREAD * (2.0 * np.pi * signed / W) ** 2)
    q = np.fft.ifft(h)
    full = q[(k[:, None] - k[None, :]) % W]
    a, b = full[:HALF, :HALF], full[:HALF, HALF:]
    tables = []
    for part in (0.5 * (a + b), 0.5 * (a - b)):
        t = part.T
        tables.append(np.stack(halves(np.block([[t.real, t.imag], [-t.imag, t.real]]))))
    return np.stack(tables)


def place(n):
    n = lax.rem(n + 2 * DEVICES, DEVICES)
    return (n // FINE, lax.rem(n, FINE))


def far_first():
    offsets = [o for o in itertools.product(range(4), range(4), range(4), range(2)) if any(o)]
    mixed = np.random.RandomState(1).permutation(len(offsets))
    offsets = [offsets[i] for i in mixed]
    return sorted(offsets, key=lambda o: -sum(min(v, 4 - v) for v in o[:3]))


def partners():
    coarse, fine = lax.axis_index("coarse"), lax.axis_index("fine")
    x, y = fine // 4, coarse // 2
    z, core = (lax.rem(fine, 4) // 2) * 2 + lax.rem(coarse, 2), lax.rem(fine, 2)
    out = []
    for dx, dy, dz, dk in far_first():
        px, py, pz, pk = lax.rem(x + dx, 4), lax.rem(y + dy, 4), lax.rem(z + dz, 4), lax.rem(core + dk, 2)
        out.append((py * 2 + lax.rem(pz, 2), px * 4 + (pz // 2) * 2 + pk))
    return out


def sincos(x):
    turns = jnp.round(x * (2.0 / np.pi))
    r = x - turns * 1.5703125
    r = r - turns * 4.837512969970703125e-4
    r = r - turns * 7.54978995489188216e-8
    z = r * r
    sine = r + r * z * (-1.6666654611e-1 + z * (8.3321608736e-3 + z * -1.9515295891e-4))
    cosine = 1.0 - 0.5 * z + z * z * (4.166664568298827e-2 + z * (-1.388731625493765e-3 + z * 2.443315711809948e-5))
    quadrant = turns.astype(jnp.int32) & 3
    odd = (quadrant & 1) == 1
    s = jnp.where(odd, cosine, sine)
    c = jnp.where(odd, sine, cosine)
    s = jnp.where(quadrant >= 2, -s, s)
    c = jnp.where((quadrant == 1) | (quadrant == 2), -c, c)
    return s, c


def spline_rows(table, r, grid, cells, shifts):
    left = (0.5 * (0.5 - shifts) * (0.5 - shifts)).astype(bf16)
    middle = (0.75 - shifts * shifts).astype(bf16)
    right = (0.5 * (0.5 + shifts) * (0.5 + shifts)).astype(bf16)
    before = ((cells - 1) & (W - 1)).astype(f32).astype(bf16)
    after = ((cells + 1) & (W - 1)).astype(f32).astype(bf16)
    at = cells.astype(f32).astype(bf16)
    none = jnp.zeros((), bf16)
    for q in range(0, P_SIZE, W):
        lanes = slice(q, q + W)
        for row in range(0, W, 64):
            rows = grid[row : row + 64, :]
            value = jnp.where(rows == before[:, lanes], left[:, lanes], none)
            value = jnp.where(rows == at[:, lanes], middle[:, lanes], value)
            value = jnp.where(rows == after[:, lanes], right[:, lanes], value)
            table[r, row : row + 64, lanes] = value


def split(g):
    hi = g.astype(bf16)
    return hi, (g - hi.astype(f32)).astype(bf16)


def whole_kernel(
    plan, field_in, phases_in, energy_in, cells_in, shifts_in, bragg_in, matrices, back, particles,
    phases, energy, cells, shifts, bragg, field, tx, ty, grid, gcells, gshifts, state, arrived, dep, cur, mright, mleft, lhs, rhs, rounded,
    sent, got, result, wave, turned, conv, operand, homes,
    small_sem, field_sem, table_sem, gs, gr, ps, pr, own_sem, s1, r1, s2, r2, hs, hr,
):
    coarse, fine = lax.axis_index("coarse"), lax.axis_index("fine")
    me = coarse * FINE + fine
    others = partners()
    slips = [plan[u] for u in range(STEPS)]
    met = [0]
    for u in range(STEPS):
        met.append(met[u] + slips[u])

    small = [
        pltpu.make_async_copy(src, dst, small_sem.at[n])
        for n, (src, dst) in enumerate((
            (cells_in, cells), (shifts_in, shifts), (phases_in, phases), (energy_in, energy), (bragg_in, bragg)))
    ]
    for copy in small:
        copy.start()
    load = pltpu.make_async_copy(field_in, field, field_sem)
    load.start()
    tables = []
    for sy in range(2):
        for n, part in enumerate((0, 1, 0)):
            tables.append(pltpu.make_async_copy(
                matrices.at[sy, part], mright.at[sy, pl.ds(n * W, W)], table_sem.at[sy, n]))
        for n, part in enumerate((0, 0, 1)):
            for bx in range(2):
                for by in range(2):
                    tables.append(pltpu.make_async_copy(
                        matrices.at[sy, part, pl.ds(by * HALF, HALF), pl.ds(bx * HALF, HALF)],
                        mleft.at[sy, pl.ds(bx * HALF, HALF), pl.ds(n * W + by * HALF, HALF)],
                        table_sem.at[sy, 3 + n * 4 + bx * 2 + by]))
    for copy in tables:
        copy.start()
    barrier = pltpu.get_barrier_semaphore()
    grid[...] = lax.broadcasted_iota(jnp.int32, (W, W), 0).astype(f32).astype(bf16)

    def build(r, carry):
        spline_rows(tx, r, grid, gcells[r, 0:1, :], gshifts[r, 0:1, :])
        spline_rows(ty, r, grid, gcells[r, 1:2, :], gshifts[r, 1:2, :])
        return carry

    for copy in small:
        copy.wait()
    gcells[0:CHAINS] = cells[...]
    gshifts[0:CHAINS] = shifts[...]
    for r in range(2):
        build(r, 0)
    load.wait()
    for copy in tables:
        copy.wait()

    def deposit(u, base, theta):
        sine, cosine = sincos(theta)
        for k in range(2):
            r = base + k + met[u]
            c, s = (GAIN * cosine[k : k + 1]).astype(bf16), (-GAIN * sine[k : k + 1]).astype(bf16)
            for row in range(0, W, 64):
                weights = tx[r, row : row + 64, :]
                dep[k, row : row + 64, :] = weights * c
                dep[k, W + row : W + row + 64, :] = weights * s
            cur[base + k] = lax.dot_general(dep[k], ty[r], (((1,), (1,)), ((), ())), preferred_element_type=f32)
        return sine, cosine

    def diffract(u, base):
        for k in range(2):
            chain = base + k
            at = me * CHAINS + chain
            keep = jnp.where((at + met[u] >= NS) & (at + met[u - 1] < NS), 0.0, 1.0) if u else None
            kept = (lambda value, keep=keep: value * keep) if u else (lambda value: value)
            for c in range(2):
                for row in range(0, HALF, 32):
                    top = kept(field[chain, c, row : row + 32, :]) + cur[chain, c * W + row : c * W + row + 32, :]
                    low = row + HALF
                    bottom = kept(field[chain, c, low : low + 32, :]) + cur[chain, c * W + low : c * W + low + 32, :]
                    for sx, v in enumerate((top + bottom, top - bottom)):
                        a, b = v[:, :HALF], v[:, HALF:]
                        rows = slice(sx * HALF + row, sx * HALF + row + 32)
                        for sy, g in enumerate((a + b, a - b)):
                            hi, lo = split(g)
                            lhs[k, sy, rows, c * HALF : c * HALF + HALF] = hi
                            lhs[k, sy, rows, W + c * HALF : W + c * HALF + HALF] = hi
                            lhs[k, sy, rows, 2 * W + c * HALF : 2 * W + c * HALF + HALF] = lo
            for sy in range(2):
                mid = jnp.dot(lhs[k, sy], mright[sy], preferred_element_type=f32)
                for sx in range(2):
                    for c in range(2):
                        hi, lo = split(mid[sx * HALF : sx * HALF + HALF, c * HALF : c * HALF + HALF])
                        cols = slice(sy * HALF, sy * HALF + HALF)
                        rhs[k, sx, c * HALF : c * HALF + HALF, cols] = hi
                        rhs[k, sx, W + c * HALF : W + c * HALF + HALF, cols] = lo
                        rhs[k, sx, 2 * W + c * HALF : 2 * W + c * HALF + HALF, cols] = hi
        for k in range(2):
            chain = base + k
            at = me * CHAINS + chain
            za = jnp.dot(mleft[0], rhs[k, 0], preferred_element_type=f32)
            zb = jnp.dot(mleft[1], rhs[k, 1], preferred_element_type=f32)
            for c in range(2):
                p, n = za[c * HALF : c * HALF + HALF], zb[c * HALF : c * HALF + HALF]
                for hx, v in enumerate((p + n, p - n)):
                    a, b = v[:, :HALF], v[:, HALF:]
                    for hy, g in enumerate((a + b, a - b)):
                        cols = slice(hy * HALF, hy * HALF + HALF)
                        rounded[chain, c * W + hx * HALF : c * W + hx * HALF + HALF, cols] = g.astype(bf16)
                        if u < STEPS - 1:
                            field[chain, c, hx * HALF : hx * HALF + HALF, cols] = g
                        else:
                            gone = (at + met[STEPS] >= NS) & (at + met[STEPS - 1] < NS)
                            sent[base + hy, pl.ds(hx * 4 + c * 2 + k, HALF, stride=8), :] = g * jnp.where(gone, 0.0, 1.0)

    def push(u, base, theta, eta, sine, cosine):
        sampled = []
        for k in range(2):
            r = base + k + met[u]
            pieces = []
            for q in range(0, P_SIZE, 256):
                picked = jnp.dot(rounded[base + k], ty[r, :, q : q + 256], preferred_element_type=f32)
                sums = [jnp.zeros((16, 256), f32) for c in range(2)]
                for row in range(0, W, 16):
                    weights = tx[r, row : row + 16, q : q + 256].astype(f32)
                    for c in range(2):
                        sums[c] = sums[c] + picked[c * W + row : c * W + row + 16] * weights
                pieces.append([jnp.sum(total, axis=0, keepdims=True) for total in sums])
            sampled.append([jnp.concatenate([piece[c] for piece in pieces], axis=1) for c in range(2)])
        first = jnp.concatenate([sampled[0][0], sampled[1][0]], axis=0)
        second = jnp.concatenate([sampled[0][1], sampled[1][1]], axis=0)
        eta = eta - 0.5 * (first * cosine - second * sine)
        state[u, 0, base : base + 2, :] = theta + eta
        state[u, 1, base : base + 2, :] = eta

    def exchange(u):
        return [
            pltpu.make_async_remote_copy(
                state.at[u, n, pl.ds(0, 2)], arrived.at[u, n], ps.at[u, n], pr.at[u, n],
                device_id=place(me - 1), device_id_type=MESH)
            for n in range(2)
        ]

    geometry = []
    for n, (src, dst) in enumerate(((cells, gcells), (shifts, gshifts))):
        geometry.append(pltpu.make_async_remote_copy(
            src, dst.at[pl.ds(4, 4)], gs.at[n], gr.at[n], device_id=place(me - 1), device_id_type=MESH))
        geometry.append(pltpu.make_async_remote_copy(
            src.at[pl.ds(0, 2)], dst.at[pl.ds(8, 2)], gs.at[n + 2], gr.at[n + 2],
            device_id=place(me - 2), device_id_type=MESH))

    def front(u):
        if not u:
            return phases[0:2], energy[0:2]
        one = slips[u - 1] == 1
        return [jnp.where(one, state[u - 1, n, 1:3, :], state[u - 1, n, 2:4, :]) for n in range(2)]

    def rear(u):
        if not u:
            return phases[2:4], energy[2:4]
        one = slips[u - 1] == 1
        return [
            jnp.where(
                one,
                jnp.concatenate([state[u - 1, n, 3:4, :], arrived[u - 1, n, 0:1, :]], axis=0),
                arrived[u - 1, n],
            )
            for n in range(2)
        ]

    moving = []
    for u in range(STEPS - 1):
        theta, eta = front(u)
        turn = deposit(u, 0, theta)
        if u == 0:
            for there in others:
                pl.semaphore_signal(barrier, inc=1, device_id=there, device_id_type=MESH)
        if u == 0:
            for r in range(2, CHAINS):
                build(r, 0)
        if u == 1:
            for copy in geometry:
                copy.wait()
            for r in range(CHAINS, REACH):
                build(r, 0)
        diffract(u, 0)
        if u == 0:
            pl.semaphore_wait(barrier, DEVICES - 1)
            for copy in geometry:
                copy.start()
        for copy in moving:
            copy.wait()
        rear_theta, rear_eta = rear(u)
        push(u, 0, theta, eta, *turn)
        rear_turn = deposit(u, 2, rear_theta)
        moving = exchange(u)
        for copy in moving:
            copy.start()
        diffract(u, 2)
        push(u, 2, rear_theta, rear_eta, *rear_turn)
    last = STEPS - 1
    def spread(src, dst, first, count, ss, rs):
        parts = pl.ds(first, count)
        for there in others:
            n = there[0] * FINE + there[1]
            pltpu.make_async_remote_copy(
                src.at[parts, pl.ds(n * 8, 8)], dst.at[parts, pl.ds(me * 8, 8)], ss, rs,
                device_id=there, device_id_type=MESH).start()

    def settle(ref, count, sem):
        view = ref.at[pl.ds(0, count), pl.ds(0, (DEVICES - 1) * 8)]
        pltpu.make_async_copy(view, view, sem).wait()

    ahead = front(last)
    ahead_turn = deposit(last, 0, ahead[0])
    diffract(last, 0)
    spread(sent, got, 0, 2, s1.at[0], r1.at[0])
    for copy in moving:
        copy.wait()
    behind = rear(last)
    behind_turn = deposit(last, 2, behind[0])
    diffract(last, 2)
    spread(sent, got, 2, 1, s1.at[1], r1.at[1])
    spread(sent, got, 3, 1, s1.at[2], r1.at[2])
    mine = pl.ds(pl.multiple_of(me * 8, 8), 8)
    for part in range(4):
        got[part, mine, :] = sent[part, mine, :]
    push(last, 0, *ahead, *ahead_turn)
    push(last, 2, *behind, *behind_turn)
    homing = [
        pltpu.make_async_remote_copy(
            state.at[last], homes.at[n], hs.at[n], hr.at[n], device_id=place(me + n + 1), device_id_type=MESH)
        for n in range(2)
    ]
    for copy in homing:
        copy.start()

    half = NS // 2
    k = lax.broadcasted_iota(jnp.int32, (1, NS), 1)
    unit = 2.0 * np.pi / NS
    turn_quad, turn_real = sincos(((k * met[STEPS]) & (NS - 1)).astype(f32) * unit)
    br, bi = bragg[0:1, :] * (1.0 / NS), bragg[1:2, :] * (1.0 / NS)
    response = jnp.concatenate([br * turn_real + bi * turn_quad, bi * turn_real - br * turn_quad], axis=0)
    hi, rest = response.astype(bf16), None
    rest = response - hi.astype(f32)
    lo = rest.astype(bf16)
    tiny = (rest - lo.astype(f32)).astype(bf16)
    down = lax.broadcasted_iota(jnp.int32, (NS, NS), 0)
    across = lax.broadcasted_iota(jnp.int32, (NS, NS), 1)
    picks = jnp.where(down == ((2 * across) & (NS - 1)) + (across >> 8), 1.0, 0.0).astype(bf16)
    ordered = (
        jnp.dot(hi, picks, preferred_element_type=f32)
        + jnp.dot(lo, picks, preferred_element_type=f32)
        + jnp.dot(tiny, picks, preferred_element_type=f32)
    )
    for parity in range(2):
        real = ordered[0:1, parity * half : parity * half + half]
        quad = ordered[1:2, parity * half : parity * half + half]

        def fill(block, carry, parity=parity, real=real, quad=quad):
            start = pl.multiple_of(block * 32, 32)
            row = lax.broadcasted_iota(jnp.int32, (32, half), 0) + start
            m = lax.broadcasted_iota(jnp.int32, (32, half), 1)
            time = (row >> 3) * 4 + ((row >> 2) & 1) * 2 + (row & 1)
            upper = (row & 2) == 0
            s, c = sincos((((2 * m + parity) * time) & (NS - 1)).astype(f32) * unit)
            wr = jnp.where(upper, c, s)
            wi = jnp.where(upper, -s, c)
            for n, (w, g) in enumerate(((wr, wr * real + wi * quad), (wi, wi * real - wr * quad))):
                cols = slice(n * half, n * half + half)
                hi, lo = split(w)
                wave[0, pl.ds(start, 32), cols] = hi
                wave[1, pl.ds(start, 32), cols] = lo
                hi, lo = split(g)
                turned[0, pl.ds(start, 32), cols] = hi
                turned[1, pl.ds(start, 32), cols] = lo
            return carry

        lax.fori_loop(0, NS // 32, fill, 0)
        dims = (((1,), (1,)), ((), ()))
        for row in range(0, NS, 256):
            rows = slice(row, row + 256)
            kernel = (
                lax.dot_general(turned[0, rows], wave[0], dims, preferred_element_type=f32)
                + lax.dot_general(turned[0, rows], wave[1], dims, preferred_element_type=f32)
                + lax.dot_general(turned[1, rows], wave[0], dims, preferred_element_type=f32)
            )
            hi, lo = split(kernel)
            conv[parity, rows, 0:NS] = hi
            conv[parity, rows, NS : 2 * NS] = hi
            conv[parity, rows, 2 * NS : 3 * NS] = lo

    mid = DEVICES // 2
    low = lax.broadcasted_iota(jnp.int32, (8, 8, HALF), 1) < 4
    settle(got, 2, r1.at[0])
    for hy in range(2):
        settle(got, 1, r1.at[1 + hy])
        for block in range(0, mid, 8):
            pieces = []
            for start in (block, mid + block):
                a = got[hy, start * 8 : start * 8 + 64, :].reshape(8, 8, HALF)
                b = got[2 + hy, start * 8 : start * 8 + 64, :].reshape(8, 8, HALF)
                pieces.append((
                    jnp.where(low, a, pltpu.roll(b, 4, 1)).reshape(64, HALF),
                    jnp.where(low, pltpu.roll(a, 4, 1), b).reshape(64, HALF),
                ))
            for hx in range(2):
                a, b = pieces[0][hx], pieces[1][hx]
                lanes = slice(hx * HALF, hx * HALF + HALF)
                rows = block * 8
                for parity, g in enumerate((a + b, a - b)):
                    hi, lo = split(g)
                    operand[parity, rows : rows + 64, lanes] = hi
                    operand[parity, NS + rows : NS + rows + 64, lanes] = lo
                    operand[parity, 2 * NS + rows : 2 * NS + rows + 64, lanes] = hi
        for row in range(0, NS, 256):
            even = jnp.dot(conv[0, row : row + 256, :], operand[0], preferred_element_type=f32)
            odd = jnp.dot(conv[1, row : row + 256, :], operand[1], preferred_element_type=f32)
            for hx in range(2):
                a, b = even[:, hx * HALF : hx * HALF + HALF], odd[:, hx * HALF : hx * HALF + HALF]
                result[2 * hy + hx, row : row + 256, :] = a + b
                result[2 * hy + hx, mid * 8 + row : mid * 8 + row + 256, :] = a - b
        spread(result, back, 2 * hy, 2, s2.at[hy], r2.at[hy])
    own = pltpu.make_async_copy(result.at[:, mine], back.at[:, mine], own_sem)
    own.start()
    for copy in homing:
        copy.wait()
    for i in range(CHAINS):
        at = i - met[last]
        for n in range(2):
            value = homes[1, n, pl.ds(jnp.clip(at + 8, 0, 3), 1), :]
            value = jnp.where(at >= -4, homes[0, n, pl.ds(jnp.clip(at + 4, 0, 3), 1), :], value)
            value = jnp.where(at >= 0, state[last, n, pl.ds(jnp.clip(at, 0, 3), 1), :], value)
            particles[i, n : n + 1, :] = value
    own.wait()
    for n, count in enumerate((2, 1, 1)):
        settle(got, count, s1.at[n])
    for hy in range(2):
        settle(got, 2, s2.at[hy])
        settle(got, 2, r2.at[hy])


def unblock_kernel(blocks, ended, out, particles, taken, staged, kept, take_sems, put_sems, end_sems):
    near, rows = [], 2 * HALF
    for q in range(4):
        near.append(pltpu.make_async_copy(
            blocks.at[:, pl.ds(q * rows, rows)], taken.at[:, pl.ds(q * rows, rows)], take_sems.at[q]))
    ends = pltpu.make_async_copy(ended, kept, end_sems.at[0])
    for copy in near:
        copy.start()
    ends.start()
    puts = []
    for q in range(4):
        near[q].wait()
        if q == 0:
            ends.wait()
            ends = pltpu.make_async_copy(kept, particles, end_sems.at[1])
            ends.start()
        for chain in range(CHAINS):
            for c in range(2):
                row = (chain // 2) * 4 + c * 2 + chain % 2
                for hx in range(2):
                    for hy in range(2):
                        staged[chain, c, hx, q * 32 : q * 32 + 32, hy * HALF : hy * HALF + HALF] = taken[
                            2 * hy + hx, pl.ds(q * rows + row, 32, stride=8), :
                        ]
        puts.append(pltpu.make_async_copy(
            staged.at[:, :, :, pl.ds(q * 32, 32)], out.at[:, :, :, pl.ds(q * 32, 32)], put_sems.at[q]))
        puts[q].start()
    for copy in puts:
        copy.wait()
    ends.wait()


def on_device(field_in, phases, energy, cell_index, offsets, slip_plan, bragg_response):
    vmem = pl.BlockSpec(memory_space=pltpu.VMEM)
    smem = pl.BlockSpec(memory_space=pltpu.SMEM)
    whole = pl.BlockSpec(memory_space=pl.ANY)
    dma = pltpu.SemaphoreType.DMA
    far = pl.BlockSpec(memory_space=pltpu.HBM)
    back, ended = pl.pallas_call(
        whole_kernel,
        out_shape=(
            jax.ShapeDtypeStruct((4, DEVICES * 8, HALF), f32),
            jax.ShapeDtypeStruct((CHAINS, 2, P_SIZE), f32),
        ),
        in_specs=[smem] + [far] * 7,
        out_specs=(whole, vmem),
        scratch_shapes=[
            pltpu.VMEM((CHAINS, P_SIZE), f32),
            pltpu.VMEM((CHAINS, P_SIZE), f32),
            pltpu.VMEM((CHAINS, 2, P_SIZE), jnp.int32),
            pltpu.VMEM((CHAINS, 2, P_SIZE), f32),
            pltpu.VMEM((2, NS), f32),
            pltpu.VMEM((CHAINS, 2, W, W), f32),
            pltpu.VMEM((REACH, W, P_SIZE), bf16),
            pltpu.VMEM((REACH, W, P_SIZE), bf16),
            pltpu.VMEM((W, W), bf16),
            pltpu.VMEM((REACH, 2, P_SIZE), jnp.int32),
            pltpu.VMEM((REACH, 2, P_SIZE), f32),
            pltpu.VMEM((STEPS, 2, CHAINS, P_SIZE), f32),
            pltpu.VMEM((STEPS, 2, 2, P_SIZE), f32),
            pltpu.VMEM((2, 2 * W, P_SIZE), bf16),
            pltpu.VMEM((CHAINS, 2 * W, W), f32),
            pltpu.VMEM((2, 3 * W, W), bf16),
            pltpu.VMEM((2, W, 3 * W), bf16),
            pltpu.VMEM((2, 2, W, 3 * W), bf16),
            pltpu.VMEM((2, 2, 3 * W, W), bf16),
            pltpu.VMEM((CHAINS, 2 * W, W), bf16),
            pltpu.VMEM((4, DEVICES * 8, HALF), f32),
            pltpu.VMEM((4, DEVICES * 8, HALF), f32),
            pltpu.VMEM((4, DEVICES * 8, HALF), f32),
            pltpu.VMEM((2, NS, NS), bf16),
            pltpu.VMEM((2, NS, NS), bf16),
            pltpu.VMEM((2, NS, 3 * NS), bf16),
            pltpu.VMEM((2, 3 * NS, W), bf16),
            pltpu.VMEM((2, 2, CHAINS, P_SIZE), f32),
            dma((5,)),
            dma,
            dma((2, 15)),
            dma((4,)),
            dma((4,)),
            dma((STEPS, 2)),
            dma((STEPS, 2)),
            dma,
            dma((3,)),
            dma((3,)),
            dma((2,)),
            dma((2,)),
            dma((2,)),
            dma((2,)),
        ],
        compiler_params=pltpu.CompilerParams(
            collective_id=0, has_side_effects=True, vmem_limit_bytes=VMEM_ALL
        ),
        name="pass",
    )(slip_plan, field_in, phases, energy, cell_index, offsets, bragg_response, jnp.asarray(diffraction_tables()))
    field_out, particles = pl.pallas_call(
        unblock_kernel,
        out_shape=(
            jax.ShapeDtypeStruct((CHAINS, 2, 2, HALF, W), f32),
            jax.ShapeDtypeStruct((CHAINS, 2, P_SIZE), f32),
        ),
        in_specs=[far, far],
        out_specs=(far, far),
        scratch_shapes=[
            pltpu.VMEM((4, DEVICES * 8, HALF), f32),
            pltpu.VMEM((CHAINS, 2, 2, HALF, W), f32),
            pltpu.VMEM((CHAINS, 2, P_SIZE), f32),
            dma((4,)),
            dma((4,)),
            dma((2,)),
        ],
        compiler_params=pltpu.CompilerParams(vmem_limit_bytes=VMEM_ALL),
        name="unblock",
    )(back, ended)
    return field_out.reshape(CHAINS, 2, W, W), particles


def solution(mesh):
    axes = ("coarse", "fine")
    in_specs = (
        P(axes, None, None, None),
        P(axes, None),
        P(axes, None),
        P(axes, None, None),
        P(axes, None, None),
        P(),
        P(),
    )
    out_specs = (P(axes, None, None, None), P(axes, None, None))
    return jax.shard_map(on_device, mesh=mesh, in_specs=in_specs, out_specs=out_specs, check_vma=False)
```

```python
import itertools

import jax
import jax.numpy as jnp
import numpy as np
from jax import lax
from jax.experimental import pallas as pl
from jax.experimental.pallas import tpu as pltpu
from jax.sharding import PartitionSpec as P

W = 256
HALF = 128
P_SIZE = 1024
STEPS = 4
NS = 512
CHAINS = 4
COARSE = 8
FINE = 16
DEVICES = COARSE * FINE
REACH = 10
GAIN = 0.25 * W * W / P_SIZE
SPREAD = 20.0
VMEM_ALL = 67043328
FLAT = pl.DeviceIdType.LOGICAL
f32, bf16 = jnp.float32, jnp.bfloat16


def halves(matrix):
    high = matrix.astype(np.float32).astype(bf16)
    low = (matrix - high.astype(np.float64)).astype(np.float32).astype(bf16)
    return high, low


def diffraction_tables():
    k = np.arange(W)
    signed = np.where(k < W // 2, k, k - W)
    h = np.exp(-1j * SPREAD * (2.0 * np.pi * signed / W) ** 2)
    q = np.fft.ifft(h)
    full = q[(k[:, None] - k[None, :]) % W]
    a, b = full[:HALF, :HALF], full[:HALF, HALF:]
    tables = []
    for part in (0.5 * (a + b), 0.5 * (a - b)):
        t = part.T
        tables.append(np.stack(halves(np.block([[t.real, t.imag], [-t.imag, t.real]]))))
    return np.stack(tables)


def place(n):
    return lax.rem(n + 2 * DEVICES, DEVICES)


def far_first():
    offsets = [o for o in itertools.product(range(4), range(4), range(4), range(2)) if any(o)]
    mixed = np.random.RandomState(1).permutation(len(offsets))
    offsets = [offsets[i] for i in mixed]
    return sorted(offsets, key=lambda o: -sum(min(v, 4 - v) for v in o[:3]))


def partners():
    coarse, fine = lax.axis_index("coarse"), lax.axis_index("fine")
    x, y = fine // 4, coarse // 2
    z, core = (lax.rem(fine, 4) // 2) * 2 + lax.rem(coarse, 2), lax.rem(fine, 2)
    def turned(v, d):
        return lax.rem(v + d, 4)

    planes = [[turned(x, dx) * 4 + turned(y, dy) * 2 * FINE for dy in range(4)] for dx in range(4)]
    depths = [lax.rem(turned(z, dz), 2) * FINE + (turned(z, dz) // 2) * 2 for dz in range(4)]
    lines = [[depth + lax.rem(core + dk, 2) for dk in range(2)] for depth in depths]
    return [planes[dx][dy] + lines[dz][dk] for dx, dy, dz, dk in far_first()]


def sincos(x):
    turns = jnp.round(x * (2.0 / np.pi))
    r = x - turns * 1.5703125
    r = r - turns * 4.837512969970703125e-4
    r = r - turns * 7.54978995489188216e-8
    z = r * r
    sine = r + r * z * (-1.6666654611e-1 + z * (8.3321608736e-3 + z * -1.9515295891e-4))
    cosine = 1.0 - 0.5 * z + z * z * (4.166664568298827e-2 + z * (-1.388731625493765e-3 + z * 2.443315711809948e-5))
    quadrant = turns.astype(jnp.int32) & 3
    odd = (quadrant & 1) == 1
    s = jnp.where(odd, cosine, sine)
    c = jnp.where(odd, sine, cosine)
    s = jnp.where(quadrant >= 2, -s, s)
    c = jnp.where((quadrant == 1) | (quadrant == 2), -c, c)
    return s, c


def spline_rows(table, r, grid, cells, shifts):
    left = (0.5 * (0.5 - shifts) * (0.5 - shifts)).astype(bf16)
    middle = (0.75 - shifts * shifts).astype(bf16)
    right = (0.5 * (0.5 + shifts) * (0.5 + shifts)).astype(bf16)
    before = ((cells - 1) & (W - 1)).astype(f32).astype(bf16)
    after = ((cells + 1) & (W - 1)).astype(f32).astype(bf16)
    at = cells.astype(f32).astype(bf16)
    none = jnp.zeros((), bf16)
    for q in range(0, P_SIZE, W):
        lanes = slice(q, q + W)
        for row in range(0, W, 64):
            rows = grid[row : row + 64, :]
            value = jnp.where(rows == before[:, lanes], left[:, lanes], none)
            value = jnp.where(rows == at[:, lanes], middle[:, lanes], value)
            value = jnp.where(rows == after[:, lanes], right[:, lanes], value)
            table[r, row : row + 64, lanes] = value


def split(g):
    hi = g.astype(bf16)
    return hi, (g - hi.astype(f32)).astype(bf16)


def whole_kernel(
    plan, field_in, phases_in, energy_in, cells_in, shifts_in, bragg_in, matrices, back, particles,
    phases, energy, cells, shifts, bragg, field, tx, ty, grid, gcells, gshifts, state, arrived, dep, cur, mright, mleft, lhs, rhs, rounded,
    sent, got, result, wave, turned, conv, operand, homes,
    small_sem, field_sem, table_sem, gs, gr, ps, pr, own_sem, s1, r1, s2, r2, hs, hr,
):
    coarse, fine = lax.axis_index("coarse"), lax.axis_index("fine")
    me = coarse * FINE + fine
    others = partners()
    slips = [plan[u] for u in range(STEPS)]
    met = [0]
    for u in range(STEPS):
        met.append(met[u] + slips[u])

    small = [
        pltpu.make_async_copy(src, dst, small_sem.at[n])
        for n, (src, dst) in enumerate((
            (cells_in, cells), (shifts_in, shifts), (phases_in, phases), (energy_in, energy), (bragg_in, bragg)))
    ]
    for copy in small:
        copy.start()
    load = pltpu.make_async_copy(field_in, field, field_sem)
    load.start()
    tables = []
    for sy in range(2):
        for n, part in enumerate((0, 1, 0)):
            tables.append(pltpu.make_async_copy(
                matrices.at[sy, part], mright.at[sy, pl.ds(n * W, W)], table_sem.at[sy, n]))
        for n, part in enumerate((0, 0, 1)):
            for bx in range(2):
                for by in range(2):
                    tables.append(pltpu.make_async_copy(
                        matrices.at[sy, part, pl.ds(by * HALF, HALF), pl.ds(bx * HALF, HALF)],
                        mleft.at[sy, pl.ds(bx * HALF, HALF), pl.ds(n * W + by * HALF, HALF)],
                        table_sem.at[sy, 3 + n * 4 + bx * 2 + by]))
    for copy in tables:
        copy.start()
    barrier = pltpu.get_barrier_semaphore()
    for there in others:
        pl.semaphore_signal(barrier, inc=1, device_id=there, device_id_type=FLAT)
    grid[...] = lax.broadcasted_iota(jnp.int32, (W, W), 0).astype(f32).astype(bf16)

    def fill_table(r, axis):
        spline_rows((tx, ty)[axis], r, grid, gcells[r, axis : axis + 1, :], gshifts[r, axis : axis + 1, :])

    for copy in small:
        copy.wait()
    gcells[0:CHAINS] = cells[...]
    gshifts[0:CHAINS] = shifts[...]
    for r in range(2):
        for axis in range(2):
            fill_table(r, axis)
    load.wait()
    for copy in tables:
        copy.wait()

    def deposit(u, base, theta):
        sine, cosine = sincos(theta)
        for k in range(2):
            r = base + k + met[u]
            c, s = (GAIN * cosine[k : k + 1]).astype(bf16), (-GAIN * sine[k : k + 1]).astype(bf16)
            for row in range(0, W, 64):
                weights = tx[r, row : row + 64, :]
                dep[k, row : row + 64, :] = weights * c
                dep[k, W + row : W + row + 64, :] = weights * s
            cur[base + k] = lax.dot_general(dep[k], ty[r], (((1,), (1,)), ((), ())), preferred_element_type=f32)
        return sine, cosine

    def diffract(u, base, slices=()):
        jobs = [(r, axis) for r in slices for axis in range(2)]

        def work():
            if jobs:
                fill_table(*jobs.pop(0))

        for k in range(2):
            chain = base + k
            at = me * CHAINS + chain
            keep = jnp.where((at + met[u] >= NS) & (at + met[u - 1] < NS), 0.0, 1.0) if u else None
            kept = (lambda value, keep=keep: value * keep) if u else (lambda value: value)
            for c in range(2):
                for row in range(0, HALF, 32):
                    top = kept(field[chain, c, row : row + 32, :]) + cur[chain, c * W + row : c * W + row + 32, :]
                    low = row + HALF
                    bottom = kept(field[chain, c, low : low + 32, :]) + cur[chain, c * W + low : c * W + low + 32, :]
                    for sx, v in enumerate((top + bottom, top - bottom)):
                        a, b = v[:, :HALF], v[:, HALF:]
                        rows = slice(sx * HALF + row, sx * HALF + row + 32)
                        for sy, g in enumerate((a + b, a - b)):
                            hi, lo = split(g)
                            lhs[k, sy, rows, c * HALF : c * HALF + HALF] = hi
                            lhs[k, sy, rows, W + c * HALF : W + c * HALF + HALF] = hi
                            lhs[k, sy, rows, 2 * W + c * HALF : 2 * W + c * HALF + HALF] = lo
            for sy in range(2):
                mid = jnp.dot(lhs[k, sy], mright[sy], preferred_element_type=f32)
                work()
                for sx in range(2):
                    for c in range(2):
                        hi, lo = split(mid[sx * HALF : sx * HALF + HALF, c * HALF : c * HALF + HALF])
                        cols = slice(sy * HALF, sy * HALF + HALF)
                        rhs[k, sx, c * HALF : c * HALF + HALF, cols] = hi
                        rhs[k, sx, W + c * HALF : W + c * HALF + HALF, cols] = lo
                        rhs[k, sx, 2 * W + c * HALF : 2 * W + c * HALF + HALF, cols] = hi
        for k in range(2):
            chain = base + k
            at = me * CHAINS + chain
            za = jnp.dot(mleft[0], rhs[k, 0], preferred_element_type=f32)
            zb = jnp.dot(mleft[1], rhs[k, 1], preferred_element_type=f32)
            work()
            for c in range(2):
                p, n = za[c * HALF : c * HALF + HALF], zb[c * HALF : c * HALF + HALF]
                for hx, v in enumerate((p + n, p - n)):
                    a, b = v[:, :HALF], v[:, HALF:]
                    for hy, g in enumerate((a + b, a - b)):
                        cols = slice(hy * HALF, hy * HALF + HALF)
                        rounded[chain, c * W + hx * HALF : c * W + hx * HALF + HALF, cols] = g.astype(bf16)
                        if u < STEPS - 1:
                            field[chain, c, hx * HALF : hx * HALF + HALF, cols] = g
                        else:
                            gone = (at + met[STEPS] >= NS) & (at + met[STEPS - 1] < NS)
                            sent[base + hy, pl.ds(hx * 4 + c * 2 + k, HALF, stride=8), :] = g * jnp.where(gone, 0.0, 1.0)

    def push(u, base, theta, eta, sine, cosine):
        sampled = []
        for k in range(2):
            r = base + k + met[u]
            pieces = []
            for q in range(0, P_SIZE, 256):
                picked = jnp.dot(rounded[base + k], ty[r, :, q : q + 256], preferred_element_type=f32)
                sums = [jnp.zeros((16, 256), f32) for c in range(2)]
                for row in range(0, W, 16):
                    weights = tx[r, row : row + 16, q : q + 256].astype(f32)
                    for c in range(2):
                        sums[c] = sums[c] + picked[c * W + row : c * W + row + 16] * weights
                pieces.append([jnp.sum(total, axis=0, keepdims=True) for total in sums])
            sampled.append([jnp.concatenate([piece[c] for piece in pieces], axis=1) for c in range(2)])
        first = jnp.concatenate([sampled[0][0], sampled[1][0]], axis=0)
        second = jnp.concatenate([sampled[0][1], sampled[1][1]], axis=0)
        eta = eta - 0.5 * (first * cosine - second * sine)
        state[u, 0, base : base + 2, :] = theta + eta
        state[u, 1, base : base + 2, :] = eta

    def exchange(u):
        return [
            pltpu.make_async_remote_copy(
                state.at[u, n, pl.ds(0, 2)], arrived.at[u, n], ps.at[u, n], pr.at[u, n],
                device_id=place(me - 1), device_id_type=FLAT)
            for n in range(2)
        ]

    geometry = []
    for n, (src, dst) in enumerate(((cells, gcells), (shifts, gshifts))):
        geometry.append(pltpu.make_async_remote_copy(
            src, dst.at[pl.ds(4, 4)], gs.at[n], gr.at[n], device_id=place(me - 1), device_id_type=FLAT))
        geometry.append(pltpu.make_async_remote_copy(
            src.at[pl.ds(0, 2)], dst.at[pl.ds(8, 2)], gs.at[n + 2], gr.at[n + 2],
            device_id=place(me - 2), device_id_type=FLAT))

    def front(u):
        if not u:
            return phases[0:2], energy[0:2]
        one = slips[u - 1] == 1
        return [jnp.where(one, state[u - 1, n, 1:3, :], state[u - 1, n, 2:4, :]) for n in range(2)]

    def rear(u):
        if not u:
            return phases[2:4], energy[2:4]
        one = slips[u - 1] == 1
        return [
            jnp.where(
                one,
                jnp.concatenate([state[u - 1, n, 3:4, :], arrived[u - 1, n, 0:1, :]], axis=0),
                arrived[u - 1, n],
            )
            for n in range(2)
        ]

    moving = []
    for u in range(STEPS - 1):
        theta, eta = front(u)
        turn = deposit(u, 0, theta)
        if u == 1:
            for copy in geometry:
                copy.wait()
        diffract(u, 0, ((2, 3), (4, 5), (7,))[u])
        if u == 0:
            pl.semaphore_wait(barrier, DEVICES - 1)
            for copy in geometry:
                copy.start()
        for copy in moving:
            copy.wait()
        rear_theta, rear_eta = rear(u)
        push(u, 0, theta, eta, *turn)
        rear_turn = deposit(u, 2, rear_theta)
        moving = exchange(u)
        for copy in moving:
            copy.start()
        diffract(u, 2, ((), (6,), (8, 9))[u])
        push(u, 2, rear_theta, rear_eta, *rear_turn)
    last = STEPS - 1
    def spread(src, dst, first, count, ss, rs):
        parts = pl.ds(first, count)
        for there in others:
            pltpu.make_async_remote_copy(
                src.at[parts, pl.ds(there * 8, 8)], dst.at[parts, pl.ds(me * 8, 8)], ss, rs,
                device_id=there, device_id_type=FLAT).start()

    def settle(ref, count, sem):
        view = ref.at[pl.ds(0, count), pl.ds(0, (DEVICES - 1) * 8)]
        pltpu.make_async_copy(view, view, sem).wait()

    ahead = front(last)
    ahead_turn = deposit(last, 0, ahead[0])
    diffract(last, 0)
    spread(sent, got, 0, 2, s1.at[0], r1.at[0])
    for copy in moving:
        copy.wait()
    behind = rear(last)
    behind_turn = deposit(last, 2, behind[0])
    diffract(last, 2)
    spread(sent, got, 2, 1, s1.at[1], r1.at[1])
    spread(sent, got, 3, 1, s1.at[2], r1.at[2])
    mine = pl.ds(pl.multiple_of(me * 8, 8), 8)
    for part in range(4):
        got[part, mine, :] = sent[part, mine, :]
    push(last, 0, *ahead, *ahead_turn)
    push(last, 2, *behind, *behind_turn)
    homing = [
        pltpu.make_async_remote_copy(
            state.at[last], homes.at[n], hs.at[n], hr.at[n], device_id=place(me + n + 1), device_id_type=FLAT)
        for n in range(2)
    ]
    for copy in homing:
        copy.start()

    half = NS // 2
    k = lax.broadcasted_iota(jnp.int32, (1, NS), 1)
    unit = 2.0 * np.pi / NS
    turn_quad, turn_real = sincos(((k * met[STEPS]) & (NS - 1)).astype(f32) * unit)
    br, bi = bragg[0:1, :] * (1.0 / NS), bragg[1:2, :] * (1.0 / NS)
    response = jnp.concatenate([br * turn_real + bi * turn_quad, bi * turn_real - br * turn_quad], axis=0)
    hi, rest = response.astype(bf16), None
    rest = response - hi.astype(f32)
    lo = rest.astype(bf16)
    tiny = (rest - lo.astype(f32)).astype(bf16)
    down = lax.broadcasted_iota(jnp.int32, (NS, NS), 0)
    across = lax.broadcasted_iota(jnp.int32, (NS, NS), 1)
    picks = jnp.where(down == ((2 * across) & (NS - 1)) + (across >> 8), 1.0, 0.0).astype(bf16)
    ordered = (
        jnp.dot(hi, picks, preferred_element_type=f32)
        + jnp.dot(lo, picks, preferred_element_type=f32)
        + jnp.dot(tiny, picks, preferred_element_type=f32)
    )
    for parity in range(2):
        real = ordered[0:1, parity * half : parity * half + half]
        quad = ordered[1:2, parity * half : parity * half + half]

        def fill(block, carry, parity=parity, real=real, quad=quad):
            start = pl.multiple_of(block * 32, 32)
            row = lax.broadcasted_iota(jnp.int32, (32, half), 0) + start
            m = lax.broadcasted_iota(jnp.int32, (32, half), 1)
            time = (row >> 3) * 4 + ((row >> 2) & 1) * 2 + (row & 1)
            upper = (row & 2) == 0
            s, c = sincos((((2 * m + parity) * time) & (NS - 1)).astype(f32) * unit)
            wr = jnp.where(upper, c, s)
            wi = jnp.where(upper, -s, c)
            for n, (w, g) in enumerate(((wr, wr * real + wi * quad), (wi, wi * real - wr * quad))):
                cols = slice(n * half, n * half + half)
                hi, lo = split(w)
                wave[0, pl.ds(start, 32), cols] = hi
                wave[1, pl.ds(start, 32), cols] = lo
                hi, lo = split(g)
                turned[0, pl.ds(start, 32), cols] = hi
                turned[1, pl.ds(start, 32), cols] = lo
            return carry

        lax.fori_loop(0, NS // 32, fill, 0)
        dims = (((1,), (1,)), ((), ()))
        for row in range(0, NS, 256):
            rows = slice(row, row + 256)
            kernel = (
                lax.dot_general(turned[0, rows], wave[0], dims, preferred_element_type=f32)
                + lax.dot_general(turned[0, rows], wave[1], dims, preferred_element_type=f32)
                + lax.dot_general(turned[1, rows], wave[0], dims, preferred_element_type=f32)
            )
            hi, lo = split(kernel)
            conv[parity, rows, 0:NS] = hi
            conv[parity, rows, NS : 2 * NS] = hi
            conv[parity, rows, 2 * NS : 3 * NS] = lo

    mid = DEVICES // 2
    low = lax.broadcasted_iota(jnp.int32, (8, 8, HALF), 1) < 4
    settle(got, 2, r1.at[0])
    for hy in range(2):
        settle(got, 1, r1.at[1 + hy])
        for block in range(0, mid, 8):
            pieces = []
            for start in (block, mid + block):
                a = got[hy, start * 8 : start * 8 + 64, :].reshape(8, 8, HALF)
                b = got[2 + hy, start * 8 : start * 8 + 64, :].reshape(8, 8, HALF)
                pieces.append((
                    jnp.where(low, a, pltpu.roll(b, 4, 1)).reshape(64, HALF),
                    jnp.where(low, pltpu.roll(a, 4, 1), b).reshape(64, HALF),
                ))
            for hx in range(2):
                a, b = pieces[0][hx], pieces[1][hx]
                lanes = slice(hx * HALF, hx * HALF + HALF)
                rows = block * 8
                for parity, g in enumerate((a + b, a - b)):
                    hi, lo = split(g)
                    operand[parity, rows : rows + 64, lanes] = hi
                    operand[parity, NS + rows : NS + rows + 64, lanes] = lo
                    operand[parity, 2 * NS + rows : 2 * NS + rows + 64, lanes] = hi
        for row in range(0, NS, 256):
            even = jnp.dot(conv[0, row : row + 256, :], operand[0], preferred_element_type=f32)
            odd = jnp.dot(conv[1, row : row + 256, :], operand[1], preferred_element_type=f32)
            for hx in range(2):
                a, b = even[:, hx * HALF : hx * HALF + HALF], odd[:, hx * HALF : hx * HALF + HALF]
                result[2 * hy + hx, row : row + 256, :] = a + b
                result[2 * hy + hx, mid * 8 + row : mid * 8 + row + 256, :] = a - b
        spread(result, back, 2 * hy, 2, s2.at[hy], r2.at[hy])
    own = pltpu.make_async_copy(result.at[:, mine], back.at[:, mine], own_sem)
    own.start()
    for copy in homing:
        copy.wait()
    for i in range(CHAINS):
        at = i - met[last]
        for n in range(2):
            value = homes[1, n, pl.ds(jnp.clip(at + 8, 0, 3), 1), :]
            value = jnp.where(at >= -4, homes[0, n, pl.ds(jnp.clip(at + 4, 0, 3), 1), :], value)
            value = jnp.where(at >= 0, state[last, n, pl.ds(jnp.clip(at, 0, 3), 1), :], value)
            particles[i, n : n + 1, :] = value
    own.wait()
    for n, count in enumerate((2, 1, 1)):
        settle(got, count, s1.at[n])
    for hy in range(2):
        settle(got, 2, s2.at[hy])
        settle(got, 2, r2.at[hy])


def unblock_kernel(blocks, ended, out, particles, taken, staged, kept, take_sems, put_sems, end_sems):
    near, rows = [], 2 * HALF
    for q in range(4):
        near.append(pltpu.make_async_copy(
            blocks.at[:, pl.ds(q * rows, rows)], taken.at[:, pl.ds(q * rows, rows)], take_sems.at[q]))
    ends = pltpu.make_async_copy(ended, kept, end_sems.at[0])
    for copy in near:
        copy.start()
    ends.start()
    puts = []
    for q in range(4):
        near[q].wait()
        if q == 0:
            ends.wait()
            ends = pltpu.make_async_copy(kept, particles, end_sems.at[1])
            ends.start()
        for chain in range(CHAINS):
            for c in range(2):
                row = (chain // 2) * 4 + c * 2 + chain % 2
                for hx in range(2):
                    for hy in range(2):
                        staged[chain, c, hx, q * 32 : q * 32 + 32, hy * HALF : hy * HALF + HALF] = taken[
                            2 * hy + hx, pl.ds(q * rows + row, 32, stride=8), :
                        ]
        puts.append(pltpu.make_async_copy(
            staged.at[:, :, :, pl.ds(q * 32, 32)], out.at[:, :, :, pl.ds(q * 32, 32)], put_sems.at[q]))
        puts[q].start()
    for copy in puts:
        copy.wait()
    ends.wait()


def on_device(field_in, phases, energy, cell_index, offsets, slip_plan, bragg_response):
    vmem = pl.BlockSpec(memory_space=pltpu.VMEM)
    smem = pl.BlockSpec(memory_space=pltpu.SMEM)
    whole = pl.BlockSpec(memory_space=pl.ANY)
    dma = pltpu.SemaphoreType.DMA
    far = pl.BlockSpec(memory_space=pltpu.HBM)
    back, ended = pl.pallas_call(
        whole_kernel,
        out_shape=(
            jax.ShapeDtypeStruct((4, DEVICES * 8, HALF), f32),
            jax.ShapeDtypeStruct((CHAINS, 2, P_SIZE), f32),
        ),
        in_specs=[smem] + [far] * 7,
        out_specs=(whole, vmem),
        scratch_shapes=[
            pltpu.VMEM((CHAINS, P_SIZE), f32),
            pltpu.VMEM((CHAINS, P_SIZE), f32),
            pltpu.VMEM((CHAINS, 2, P_SIZE), jnp.int32),
            pltpu.VMEM((CHAINS, 2, P_SIZE), f32),
            pltpu.VMEM((2, NS), f32),
            pltpu.VMEM((CHAINS, 2, W, W), f32),
            pltpu.VMEM((REACH, W, P_SIZE), bf16),
            pltpu.VMEM((REACH, W, P_SIZE), bf16),
            pltpu.VMEM((W, W), bf16),
            pltpu.VMEM((REACH, 2, P_SIZE), jnp.int32),
            pltpu.VMEM((REACH, 2, P_SIZE), f32),
            pltpu.VMEM((STEPS, 2, CHAINS, P_SIZE), f32),
            pltpu.VMEM((STEPS, 2, 2, P_SIZE), f32),
            pltpu.VMEM((2, 2 * W, P_SIZE), bf16),
            pltpu.VMEM((CHAINS, 2 * W, W), f32),
            pltpu.VMEM((2, 3 * W, W), bf16),
            pltpu.VMEM((2, W, 3 * W), bf16),
            pltpu.VMEM((2, 2, W, 3 * W), bf16),
            pltpu.VMEM((2, 2, 3 * W, W), bf16),
            pltpu.VMEM((CHAINS, 2 * W, W), bf16),
            pltpu.VMEM((4, DEVICES * 8, HALF), f32),
            pltpu.VMEM((4, DEVICES * 8, HALF), f32),
            pltpu.VMEM((4, DEVICES * 8, HALF), f32),
            pltpu.VMEM((2, NS, NS), bf16),
            pltpu.VMEM((2, NS, NS), bf16),
            pltpu.VMEM((2, NS, 3 * NS), bf16),
            pltpu.VMEM((2, 3 * NS, W), bf16),
            pltpu.VMEM((2, 2, CHAINS, P_SIZE), f32),
            dma((5,)),
            dma,
            dma((2, 15)),
            dma((4,)),
            dma((4,)),
            dma((STEPS, 2)),
            dma((STEPS, 2)),
            dma,
            dma((3,)),
            dma((3,)),
            dma((2,)),
            dma((2,)),
            dma((2,)),
            dma((2,)),
        ],
        compiler_params=pltpu.CompilerParams(
            collective_id=0, has_side_effects=True, vmem_limit_bytes=VMEM_ALL
        ),
        name="pass",
    )(slip_plan, field_in, phases, energy, cell_index, offsets, bragg_response, jnp.asarray(diffraction_tables()))
    field_out, particles = pl.pallas_call(
        unblock_kernel,
        out_shape=(
            jax.ShapeDtypeStruct((CHAINS, 2, 2, HALF, W), f32),
            jax.ShapeDtypeStruct((CHAINS, 2, P_SIZE), f32),
        ),
        in_specs=[far, far],
        out_specs=(far, far),
        scratch_shapes=[
            pltpu.VMEM((4, DEVICES * 8, HALF), f32),
            pltpu.VMEM((CHAINS, 2, 2, HALF, W), f32),
            pltpu.VMEM((CHAINS, 2, P_SIZE), f32),
            dma((4,)),
            dma((4,)),
            dma((2,)),
        ],
        compiler_params=pltpu.CompilerParams(vmem_limit_bytes=VMEM_ALL),
        name="unblock",
    )(back, ended)
    return field_out.reshape(CHAINS, 2, W, W), particles


def solution(mesh):
    axes = ("coarse", "fine")
    in_specs = (
        P(axes, None, None, None),
        P(axes, None),
        P(axes, None),
        P(axes, None, None),
        P(axes, None, None),
        P(),
        P(),
    )
    out_specs = (P(axes, None, None, None), P(axes, None, None))
    return jax.shard_map(on_device, mesh=mesh, in_specs=in_specs, out_specs=out_specs, check_vma=False)
```
